512 devices in a mesh: lon: 64 (over z, x, y_lo), lat: 8 (over y_hi, core).
Axes of the slice: x: 4, y: 8 (y_hi: 4, y_lo: 2; y = y_hi * 2 + y_lo), z: 8, core: 2. Of those that a mesh axis runs over, the one named last changes fastest.
Arguments:
- inputs: bfloat16 [64, 2048, 256], P('lat', 'lon'), may hold values from -6 to 6
- psi_raw: float32 [4, 64, 3, 257], P(None, 'lat'), may hold values from -6 to 6
- widths: int32 [64], P('lat'), may hold values from 1 to 4, as said below
- w_group: bfloat16 [4, 4, 256], replicated, may hold values from -1.5 to 1.5
- w_mix: bfloat16 [256, 256], replicated, may hold values from -0.375 to 0.375
- grad_out: bfloat16 [64, 2048, 256], P('lat', 'lon'), may hold values from -6 to 6
Outputs:
- outputs: bfloat16 [64, 2048, 256], P('lat', 'lon')
- grad_in: bfloat16 [64, 2048, 256], P('lat', 'lon')
The draws below stay inside these ranges and needn't reach their ends.
Inputs may be any that keep to these rules, and one draw needn't show every extreme that they name: `widths`: let d be a row's distance to the nearer pole (min(i, 63 - i)). A row's width is at most min(4, max(1, 2 * 4 // (d + 1)) + 1); the row nearest each pole has width 4.
All inputs are finite; a program needn't handle non-finite values.
Results may differ from the reference program's by a relative error of at most 0.011.
Values may be sent and summed in bfloat16 or wider, within the bound.
A program may use at most 192 MiB of HBM per device.

```python
from functools import partial
import jax
import jax.numpy as jnp
from jax import lax

C = 256
K = 4
GROUP = 4
SMAX = 4
LON_DEV = 32
TAPS = 257
NLAT = 64
NLON = 2048


def draw_widths(key, part):
    row_index = jnp.arange(NLAT, dtype=jnp.int32)
    distance = jnp.minimum(row_index, NLAT - 1 - row_index)
    bound = jnp.minimum(SMAX, jnp.maximum(1, 2 * SMAX // (distance + 1)) + 1)
    chosen = jax.random.randint(key, (NLAT,), 0, 1 << 20, dtype=jnp.int32)
    drawn = 1 + chosen % bound
    return jnp.where(distance == 0, SMAX, drawn).astype(jnp.int32)


def level_of(key, extent, cuts, low, high):
    def one(dim, blocks):
        draws = jax.random.uniform(jax.random.fold_in(jax.random.fold_in(key, 6), dim), (blocks,), jnp.float32, low / len(cuts), high / len(cuts))
        return jnp.repeat(jnp.exp(draws), extent[dim] // blocks).reshape((-1,) + (1,) * (len(extent) - dim - 1))

    factor_of = one(*cuts[0])
    for cut in cuts[1:]:
        factor_of = factor_of * one(*cut)
    return factor_of


def gaussian(key, dims, scale, most, shards=(), kind=jnp.bfloat16):
    values = jax.random.normal(key, dims, jnp.float32) * scale
    if len(shards) > 0:
        values = level_of(key, dims, shards, -0.22, 0.18) * values
    return jnp.clip(values, min=-most, max=most).astype(kind)


def setup_inputs(seed: int = 0) -> dict:
    seeds = jax.random.split(jax.random.key(seed), 7)
    return {
        "inputs": gaussian(seeds[0], (NLAT, NLON, C), 1.0, 6.0, ((0, 8), (1, 64))),
        "psi_raw": gaussian(seeds[1], (K, NLAT, 3, TAPS), 1.0, 6.0, ((1, 8),), jnp.float32),
        "widths": draw_widths(jax.random.fold_in(seeds[6], 71), 0),
        "w_group": gaussian(seeds[3], (K, GROUP, C), (K * GROUP) ** -0.5, 1.5),
        "w_mix": gaussian(seeds[4], (C, C), C ** -0.5, 0.375),
        "grad_out": gaussian(seeds[5], (NLAT, NLON, C), 1.0, 6.0, ((0, 8), (1, 64))),
    }


def masked_filter(psi_raw, widths):
    taps = psi_raw.shape[-1]
    offset = jnp.arange(taps, dtype=jnp.int32) - SMAX * LON_DEV
    reach = widths.astype(jnp.int32)[:, None] * LON_DEV
    keep = (jnp.abs(offset)[None, :] <= reach).astype(jnp.float32)
    scale = lax.rsqrt(3.0 * (2.0 * reach.astype(jnp.float32) + 1.0))
    return (psi_raw * (keep * scale)[None, :, None, :]).astype(jnp.bfloat16)

def correlate(rows_data, filters):
    count = rows_data.shape[1]
    taps = filters.shape[-1]
    places = ((SMAX * LON_DEV - jnp.arange(taps, dtype=jnp.int32)) % count).astype(jnp.int32)
    kernel = jnp.zeros(filters.shape[:-1] + (count,), filters.dtype).at[..., places].set(filters)
    spectrum = jnp.fft.rfft(rows_data, axis=1)
    response = jnp.fft.rfft(kernel, axis=-1)
    combined = jnp.einsum('baf,afc->bfc', response, spectrum)
    return jnp.fft.irfft(combined, n=count, axis=1)

def reference(inputs, psi_raw, widths, w_group, w_mix, grad_out):
    filters = masked_filter(psi_raw, widths).astype(jnp.float32)
    padded_in = jnp.pad(inputs, ((1, 1), (0, 0), (0, 0)))
    grouped_w = w_group.astype(jnp.float32).reshape(K, GROUP, C // GROUP, GROUP)
    activation = partial(jax.nn.gelu, approximate=True)

    def forward_row(index):
        rows_data = lax.dynamic_slice_in_dim(padded_in, index, 3, 0).astype(jnp.float32)
        row_filters = lax.dynamic_slice_in_dim(filters, index, 1, 1)[:, 0]
        convolved = correlate(rows_data, row_filters).astype(jnp.bfloat16)
        convolved = lax.optimization_barrier(convolved).astype(jnp.float32)
        split_conv = convolved.reshape(K, NLON, C // GROUP, GROUP)
        mixed_in = jnp.einsum('kjgq,kqgs->jgs', split_conv, grouped_w)
        mixed_in = mixed_in.astype(jnp.bfloat16).reshape(NLON, C)
        pre_act = jnp.dot(mixed_in, w_mix, preferred_element_type=jnp.float32)
        outputs = activation(pre_act).astype(jnp.bfloat16)
        _, backward = jax.vjp(activation, pre_act)
        cotangent = lax.dynamic_slice_in_dim(grad_out, index, 1, 0)[0].astype(jnp.float32)
        grad_pre, = backward(cotangent)
        grad_mixed = lax.dot_general(grad_pre.astype(jnp.bfloat16), w_mix, (((1,), (1,)), ((), ())), preferred_element_type=jnp.float32)
        return (outputs, grad_mixed.astype(jnp.bfloat16))
    outputs, grad_mixed = lax.map(forward_row, jnp.arange(NLAT, dtype=jnp.int32))
    padded_grad = jnp.pad(grad_mixed, ((1, 1), (0, 0), (0, 0)))
    flipped = jnp.pad(jnp.flip(filters, axis=3), ((0, 0), (1, 1), (0, 0), (0, 0)))

    def backward_row(index):
        grads = lax.dynamic_slice_in_dim(padded_grad, index, 3, 0).astype(jnp.float32)
        spread = jnp.einsum('ajgs,kqgs->akjgq', grads.reshape(3, NLON, C // GROUP, GROUP), grouped_w)
        spread = lax.optimization_barrier(spread.astype(jnp.bfloat16)).astype(jnp.float32)
        spread = spread.reshape(3, K, NLON, C)
        window = lax.dynamic_slice_in_dim(flipped, index, 3, 1)
        chosen = jnp.stack([window[:, 2 - row_tap, row_tap] for row_tap in range(3)], axis=0)
        sources = jnp.stack([spread[2 - row_tap] for row_tap in range(3)], axis=0)
        result = correlate(sources.reshape(3 * K, NLON, C), chosen.reshape(1, 3 * K, chosen.shape[-1]))
        return result[0].astype(jnp.bfloat16)
    grad_in = lax.map(backward_row, jnp.arange(NLAT, dtype=jnp.int32))
    return (outputs, grad_in)
```

```python
import functools

import jax
import jax.numpy as jnp
from jax import lax
from jax.experimental import pallas as pl
from jax.experimental.pallas import tpu as pltpu
from jax.sharding import PartitionSpec as P

GROUP = 4
SMAX = 4
LANES = 384
CHUNKS = 4
NEAR = (-1, 1, -2, 2)
FAR = (-3, 3, -4, 4)
SLOT = {-2: 0, -1: 1, 0: 2, 1: 3, 2: 4}
FAR_SLOT = {-4: 0, -3: 1, 3: 2, 4: 3}
MESH = pl.DeviceIdType.MESH
F32 = jnp.float32
BF16 = jnp.bfloat16


def iota(shape, axis):
    return lax.broadcasted_iota(jnp.int32, shape, axis)


def kernel(
    n_lon, n_lat,
    x_hbm, psi_hbm, widths, wg_hbm, wm_hbm, go_hbm,
    out_ref, gin_ref,
    psi, wg, wm, go, xw, gw, xe, ge, ff, fr, tf, tb, te, tbe, wbd, cv, acc,
    local_sem, send_sem, recv_sem,
):
    rows, lon_dev, channels = x_hbm.shape
    kernels, taps = psi_hbm.shape[0], psi_hbm.shape[3]
    centre = SMAX * lon_dev
    per = rows // CHUNKS
    wide = lon_dev * 5
    lon, lat = lax.axis_index("lon"), lax.axis_index("lat")
    north, south = lat == 0, lat == n_lat - 1

    def at_lon(by):
        return lax.rem(lon + (by + n_lon), n_lon)

    barrier = pltpu.get_barrier_semaphore()

    def greet(by, up):
        pl.semaphore_signal(
            barrier, inc=1, device_id={"lon": at_lon(by), "lat": lat + up}, device_id_type=MESH
        )

    for by in NEAR:
        greet(by, 0)

    @pl.when(jnp.logical_not(north))
    def _():
        for by in (0,) + NEAR:
            greet(by, -1)

    @pl.when(jnp.logical_not(south))
    def _():
        for by in (0,) + NEAR:
            greet(by, 1)

    polar = jnp.logical_or(north, south)

    @pl.when(polar)
    def _():
        for by in FAR:
            greet(by, 0)

    own = pl.ds(SLOT[0] * lon_dev, lon_dev)
    locals_ = [
        pltpu.make_async_copy(psi_hbm, psi, local_sem.at[0]),
        pltpu.make_async_copy(wg_hbm, wg, local_sem.at[1]),
        pltpu.make_async_copy(wm_hbm, wm, local_sem.at[2]),
        pltpu.make_async_copy(go_hbm, go, local_sem.at[3]),
        pltpu.make_async_copy(x_hbm, xw.at[pl.ds(1, rows), own, :], local_sem.at[4]),
    ]
    for copy in locals_:
        copy.start()

    locals_[0].wait()
    ff[...] = jnp.zeros_like(ff)
    lane = iota((1, taps), 1)
    for i in range(rows):
        reach = widths[i] * lon_dev
        span = jnp.full((1, taps), 3.0 * (2.0 * reach.astype(F32) + 1.0), F32)
        keep = jnp.where(jnp.abs(lane - centre) <= reach, lax.rsqrt(span), 0.0)
        for k in range(kernels):
            ff[i, k, 0:3, 0:taps] = psi[k, i] * keep

    def near_copy(phase, source, at, buf, index, by, up, row, count, target):
        return pltpu.make_async_remote_copy(
            src_ref=source.at[pl.ds(row, count), at, :],
            dst_ref=buf.at[pl.ds(target, count), pl.ds(SLOT[-by] * lon_dev, lon_dev), :],
            send_sem=send_sem.at[phase, index],
            recv_sem=recv_sem.at[phase, index],
            device_id={"lon": at_lon(by), "lat": lat + up},
            device_id_type=MESH,
        )

    def chunk_copies(phase, source, first, at, buf, c):
        return [
            near_copy(phase, source, at, buf, c * 4 + n, by, 0, first + c * per, per, 1 + c * per)
            for n, by in enumerate(NEAR)
        ]

    def edge_copies(phase, source, first, at, buf, up):
        base = 4 * CHUNKS + (0 if up < 0 else 5)
        row, target = (first, rows + 1) if up < 0 else (first + rows - 1, 0)
        return [
            near_copy(phase, source, at, buf, base + n, by, up, row, 1, target)
            for n, by in enumerate((0,) + NEAR)
        ]

    far_rows = ((0, {3: 5, 4: 3}), (1, {3: 4, 4: 2}))

    def far_copies(phase, source, first, at, buf, pole):
        counts = far_rows[phase][1]
        found = []
        for n, by in enumerate(FAR):
            count = counts[abs(by)]
            row = 0 if pole == 0 else rows - count
            found.append(
                pltpu.make_async_remote_copy(
                    src_ref=source.at[pl.ds(first + row, count), at, :],
                    dst_ref=buf.at[
                        pl.ds(1 + row, count), pl.ds(FAR_SLOT[-by] * lon_dev, lon_dev), :
                    ],
                    send_sem=send_sem.at[phase, 4 * CHUNKS + 10 + n],
                    recv_sem=recv_sem.at[phase, 4 * CHUNKS + 10 + n],
                    device_id={"lon": at_lon(by), "lat": lat},
                    device_id_type=MESH,
                )
            )
        return found

    every = pl.ds(0, lon_dev)
    forward = (0, x_hbm, 0, every, xw)
    backward = (1, gw, 1, own, gw)
    forward_far = (0, x_hbm, 0, every, xe)
    backward_far = (1, gw, 1, own, ge)
    inner = (jnp.logical_not(north), jnp.logical_not(south))

    def run(copies, what):
        for copy in copies:
            getattr(copy, what)()

    def edges(phase_args, up, what):
        ok = inner[0] if up < 0 else inner[1]
        if what == "wait_recv":
            ok = inner[1] if up < 0 else inner[0]

        @pl.when(ok)
        def _():
            run(edge_copies(*phase_args, up), what)

    def fars(far_args, pole, what):
        @pl.when(north if pole == 0 else south)
        def _():
            run(far_copies(*far_args, pole), what)

    expected = (
        4
        + 5 * inner[0].astype(jnp.int32)
        + 5 * inner[1].astype(jnp.int32)
        + 4 * polar.astype(jnp.int32)
    )
    pl.semaphore_wait(barrier, expected)

    edges(forward, 1, "start")
    run(chunk_copies(*forward, 0), "start")
    edges(forward, -1, "start")
    for pole in (0, 1):
        fars(forward_far, pole, "start")
    for c in range(1, CHUNKS):
        run(chunk_copies(*forward, c), "start")

    flip = jnp.where(
        iota((LANES, LANES), 0) + iota((LANES, LANES), 1) == 2 * centre, 1.0, 0.0
    ).astype(BF16)
    flipped = jnp.dot(
        ff[...].reshape(rows * kernels * 8, LANES).astype(BF16), flip, preferred_element_type=F32
    )
    fr[pl.ds(1, rows)] = flipped.reshape(rows, kernels, 8, LANES)

    def filter_copy(up):
        n = 4 * CHUNKS + 14 + (0 if up < 0 else 1)
        row, target = (1, rows + 1) if up < 0 else (rows, 0)
        return pltpu.make_async_remote_copy(
            src_ref=fr.at[row],
            dst_ref=fr.at[target],
            send_sem=send_sem.at[0, n],
            recv_sem=recv_sem.at[0, n],
            device_id={"lon": lon, "lat": lat + up},
            device_id_type=MESH,
        )

    @pl.when(inner[0])
    def _():
        filter_copy(-1).start()

    @pl.when(inner[1])
    def _():
        filter_copy(1).start()

    blank = jnp.zeros((wide, channels), BF16)

    @pl.when(north)
    def _():
        xw[0] = blank
        gw[0] = blank
        fr[0] = jnp.zeros(fr.shape[1:], F32)

    @pl.when(south)
    def _():
        xw[rows + 1] = blank
        gw[rows + 1] = blank
        fr[rows + 1] = jnp.zeros(fr.shape[1:], F32)

    def near_block(filters, row, t, k):
        base = jnp.broadcast_to(filters[row, k, t : t + 1, 0:256], (lon_dev, 256))
        return pltpu.roll(base, 256 - 2 * lon_dev, 1, stride=1, stride_axis=0).astype(BF16)

    def far_block(filters, row, t, k):
        lane = iota((lon_dev, 128), 1)

        def part(first):
            return jnp.broadcast_to(
                filters[row, k, t : t + 1, first : first + 128], (lon_dev, 128)
            )

        low = jnp.where(lane < 2 * lon_dev, part(0), 0.0)
        high = jnp.where(lane > 2 * lon_dev, part(128), part(256))
        low = pltpu.roll(low, 0, 1, stride=1, stride_axis=0)
        high = pltpu.roll(high, 128 - lon_dev, 1, stride=1, stride_axis=0)
        return jnp.where(lane < 2 * lon_dev, low, high).astype(BF16)

    def put(dst, index, k, block):
        dst[index, pl.ds(k * lon_dev, lon_dev), :] = block

    @pl.loop(0, rows)
    def _(i):
        for t in range(3):
            for k in range(kernels):
                put(tf, i * 3 + t, k, near_block(ff, i, t, k))

    locals_[1].wait()
    inside = (iota((channels, channels), 0) // GROUP) == (iota((channels, channels), 1) // GROUP)
    for k in range(kernels):
        four = wg[k].astype(F32)
        eight = jnp.concatenate([four, four], axis=0)
        full = jnp.broadcast_to(eight[None], (channels // 8, 8, channels))
        full = full.reshape(channels, channels)
        wbd[pl.ds(k * channels, channels), :] = jnp.where(inside, full, 0.0).astype(BF16)

    for pole in (0, 1):

        @pl.when(north if pole == 0 else south)
        def _():
            for a in range(4):
                row = a if pole == 0 else rows - 1 - a
                for t in range(3):
                    for k in range(kernels):
                        put(te, a * 3 + t, k, far_block(ff, row, t, k))
                        put(tbe, a * 3 + t, k, far_block(fr, row + 1, t, k))

    @pl.when(inner[1])
    def _():
        filter_copy(-1).wait_recv()

    @pl.when(inner[0])
    def _():
        filter_copy(1).wait_recv()

    @pl.loop(0, rows)
    def _(i):
        for t in range(3):
            for k in range(kernels):
                put(tb, i * 3 + t, k, near_block(fr, i + 2 - t, t, k))

    for copy in locals_[2:]:
        copy.wait()

    def far_terms(table, index, buf, row, zero_far):
        if zero_far:
            return jnp.dot(
                table[index, :, lon_dev : 3 * lon_dev],
                buf[row, lon_dev : 3 * lon_dev, :],
                preferred_element_type=F32,
            )
        return jnp.dot(table[index], buf[row], preferred_element_type=F32)

    def conv(table, buf, row_of, c):
        for n in range(per):
            i = c * per + n
            total = None
            for t in range(3):
                term = jnp.dot(
                    table[i * 3 + t, :, 0:wide], buf[row_of(i, t)], preferred_element_type=F32
                )
                total = term if total is None else total + term
            acc[n] = total

    def mix_in(c):
        for n in range(per):
            for k in range(kernels):
                cv[pl.ds(n * lon_dev, lon_dev), pl.ds(k * channels, channels)] = acc[
                    n, pl.ds(k * lon_dev, lon_dev), :
                ].astype(BF16)

    root = 0.7978845608028654
    cubic = 0.044715

    arrived = set()

    def need(phase_args, chunks):
        for c in chunks:
            key = (phase_args[0], c)
            if 0 <= c < CHUNKS and key not in arrived:
                arrived.add(key)
                run(chunk_copies(*phase_args, c), "wait_recv")
            if c == -1:
                edges(phase_args, 1, "wait_recv")
            if c == CHUNKS:
                edges(phase_args, -1, "wait_recv")

    for c in range(CHUNKS):
        need(forward, (c - 1, c, c + 1))
        conv(tf, xw, lambda i, t: i + t, c)
        for pole in (0, 1):
            found = []
            for n in range(per):
                i = c * per + n
                a = i if pole == 0 else rows - 1 - i
                for t in range(3):
                    source = i + t - 1
                    far = source if pole == 0 else rows - 1 - source
                    if a < 4 and far >= 0:
                        found.append((n, a, t, source))
            if not found:
                continue

            @pl.when(north if pole == 0 else south)
            def _():
                if c == (0 if pole == 0 else CHUNKS // 2):
                    run(far_copies(*forward_far, pole), "wait_recv")
                for n, a, t, source in found:
                    acc[n] += far_terms(te, a * 3 + t, xe, source + 1, a >= 2)

        mix_in(c)
        mixed = jnp.dot(cv[...], wbd[...], preferred_element_type=F32).astype(BF16)
        v = jnp.dot(mixed, wm[...], preferred_element_type=F32)
        square = v * v
        th = jnp.tanh(root * v * (1.0 + cubic * square))
        half = 0.5 * (1.0 + th)
        mine = pl.ds(c * per, per)
        shape = (per, lon_dev, channels)
        out_ref[mine] = (v * half).astype(BF16).reshape(shape)
        slope = half + 0.5 * v * (1.0 - th * th) * (root * (1.0 + 3.0 * cubic * square))
        pulled = go[mine].astype(F32).reshape(per * lon_dev, channels) * slope
        back = lax.dot_general(
            pulled.astype(BF16), wm[...], (((1,), (1,)), ((), ())), preferred_element_type=F32
        )
        gw[pl.ds(1 + c * per, per), own, :] = back.astype(BF16).reshape(shape)
        run(chunk_copies(*backward, c), "start")
        if c == 0:
            edges(backward, -1, "start")
        if c == CHUNKS // 2 - 1:
            fars(backward_far, 0, "start")
        if c == CHUNKS - 1:
            edges(backward, 1, "start")
            fars(backward_far, 1, "start")

    for c in (1, 2, 0, 3):
        need(backward, (c - 1, c, c + 1))
        conv(tb, gw, lambda i, t: i + 2 - t, c)
        for pole in (0, 1):
            found = []
            for n in range(per):
                i = c * per + n
                for t in range(3):
                    source = i + 1 - t
                    far = source if pole == 0 else rows - 1 - source
                    if 0 <= far < 4:
                        found.append((n, far, t, source))
            if not found:
                continue

            @pl.when(north if pole == 0 else south)
            def _():
                if c == 1:
                    run(far_copies(*backward_far, pole), "wait_recv")
                for n, a, t, source in found:
                    acc[n] += far_terms(tbe, a * 3 + t, ge, source + 1, a >= 2)

        mix_in(c)
        total = None
        for k in range(kernels):
            at = pl.ds(k * channels, channels)
            term = lax.dot_general(
                cv[:, at], wbd[at, :], (((1,), (1,)), ((), ())), preferred_element_type=F32
            )
            total = term if total is None else total + term
        gin_ref[pl.ds(c * per, per)] = total.astype(BF16).reshape(per, lon_dev, channels)

    for args, far_args in ((forward, forward_far), (backward, backward_far)):
        for c in range(CHUNKS):
            run(chunk_copies(*args, c), "wait_send")
        for up in (-1, 1):
            edges(args, up, "wait_send")
        for pole in (0, 1):
            fars(far_args, pole, "wait_send")

    @pl.when(inner[0])
    def _():
        filter_copy(-1).wait_send()

    @pl.when(inner[1])
    def _():
        filter_copy(1).wait_send()


def body(n_lon, n_lat, inputs, psi_raw, widths, w_group, w_mix, grad_out):
    rows, lon_dev, channels = inputs.shape
    kernels = psi_raw.shape[0]
    wide = 5 * lon_dev
    depth = kernels * lon_dev
    per = rows // CHUNKS
    copies = 4 * CHUNKS + 16
    anywhere = pl.BlockSpec(memory_space=pl.ANY)
    vmem = pl.BlockSpec(memory_space=pltpu.VMEM)
    shape = jax.ShapeDtypeStruct(inputs.shape, BF16)
    return pl.pallas_call(
        functools.partial(kernel, n_lon, n_lat),
        name="disco",
        out_shape=(shape, shape),
        in_specs=[
            anywhere, anywhere, pl.BlockSpec(memory_space=pltpu.SMEM),
            anywhere, anywhere, anywhere,
        ],
        out_specs=(vmem, vmem),
        scratch_shapes=[
            pltpu.VMEM(psi_raw.shape, F32),
            pltpu.VMEM(w_group.shape, BF16),
            pltpu.VMEM(w_mix.shape, BF16),
            pltpu.VMEM(grad_out.shape, BF16),
            pltpu.VMEM((rows + 2, wide, channels), BF16),
            pltpu.VMEM((rows + 2, wide, channels), BF16),
            pltpu.VMEM((rows + 2, 4 * lon_dev, channels), BF16),
            pltpu.VMEM((rows + 2, 4 * lon_dev, channels), BF16),
            pltpu.VMEM((rows, kernels, 8, LANES), F32),
            pltpu.VMEM((rows + 2, kernels, 8, LANES), F32),
            pltpu.VMEM((rows * 3, depth, 256), BF16),
            pltpu.VMEM((rows * 3, depth, 256), BF16),
            pltpu.VMEM((12, depth, 4 * lon_dev), BF16),
            pltpu.VMEM((12, depth, 4 * lon_dev), BF16),
            pltpu.VMEM((kernels * channels, channels), BF16),
            pltpu.VMEM((per * lon_dev, kernels * channels), BF16),
            pltpu.VMEM((per, depth, channels), F32),
            pltpu.SemaphoreType.DMA((5,)),
            pltpu.SemaphoreType.DMA((2, copies)),
            pltpu.SemaphoreType.DMA((2, copies)),
        ],
        compiler_params=pltpu.CompilerParams(
            collective_id=0, has_side_effects=True, vmem_limit_bytes=40 * 1024 * 1024
        ),
        cost_estimate=pl.CostEstimate(
            flops=4_000_000_000, bytes_accessed=2_000_000, transcendentals=65536
        ),
    )(inputs, psi_raw, widths, w_group, w_mix, grad_out)


def solution(mesh):
    return jax.shard_map(
        functools.partial(body, mesh.shape["lon"], mesh.shape["lat"]),
        mesh=mesh,
        in_specs=(
            P("lat", "lon", None),
            P(None, "lat", None, None),
            P("lat"),
            P(),
            P(),
            P("lat", "lon", None),
        ),
        out_specs=(P("lat", "lon", None), P("lat", "lon", None)),
        check_vma=False,
    )
```

```python
import functools

import jax
import jax.numpy as jnp
from jax import lax
from jax.experimental import pallas as pl
from jax.experimental.pallas import tpu as pltpu
from jax.sharding import PartitionSpec as P

GROUP = 4
SMAX = 4
LANES = 384
NEAR = (-1, 1, -2, 2)
FAR = (-3, 3, -4, 4)
SLOT = {-2: 0, -1: 1, 0: 2, 1: 3, 2: 4}
FAR_SLOT = {-4: 0, -3: 1, 3: 2, 4: 3}
MESH = pl.DeviceIdType.MESH
F32 = jnp.float32
BF16 = jnp.bfloat16


def iota(shape, axis):
    return lax.broadcasted_iota(jnp.int32, shape, axis)


def kernel(
    n_lon, n_lat,
    x_hbm, psi_hbm, widths, wg_hbm, wm_hbm, go_hbm,
    out_ref, gin_ref,
    psi, wg, wm, go, xw, gw, xe, ge, ff, fr, fsend, frecv, tf, tb, te, tbe, wbd, cv, acc,
    local_sem, send_sem, recv_sem,
):
    rows, lon_dev, channels = x_hbm.shape
    kernels, taps = psi_hbm.shape[0], psi_hbm.shape[3]
    centre = SMAX * lon_dev
    wide = lon_dev * 5
    lon, lat = lax.axis_index("lon"), lax.axis_index("lat")
    north, south = lat == 0, lat == n_lat - 1
    polar = jnp.logical_or(north, south)
    above, below = jnp.logical_not(north), jnp.logical_not(south)

    def at_lon(by):
        return lax.rem(lon + (by + n_lon), n_lon)

    barrier = pltpu.get_barrier_semaphore()

    def greet(by, up):
        pl.semaphore_signal(
            barrier, inc=1, device_id={"lon": at_lon(by), "lat": lat + up}, device_id_type=MESH
        )

    for by in NEAR:
        greet(by, 0)

    @pl.when(above)
    def _():
        greet(0, -1)

    @pl.when(below)
    def _():
        greet(0, 1)

    @pl.when(polar)
    def _():
        for by in FAR:
            greet(by, 0)

    own = pl.ds(SLOT[0] * lon_dev, lon_dev)
    every = pl.ds(0, lon_dev)
    locals_ = [
        pltpu.make_async_copy(psi_hbm, psi, local_sem.at[0]),
        pltpu.make_async_copy(wg_hbm, wg, local_sem.at[1]),
        pltpu.make_async_copy(wm_hbm, wm, local_sem.at[2]),
        pltpu.make_async_copy(go_hbm, go, local_sem.at[3]),
        pltpu.make_async_copy(x_hbm, xw.at[pl.ds(1, rows), own, :], local_sem.at[4]),
    ]
    for copy in locals_:
        copy.start()

    side = 1 - 2 * lax.rem(lon, 2)

    def slot_at(by):
        return pl.ds(pl.multiple_of((by + 2) * lon_dev, lon_dev), lon_dev)

    def remote(phase, index, src, dst, by, up=0):
        return pltpu.make_async_remote_copy(
            src_ref=src,
            dst_ref=dst,
            send_sem=send_sem.at[phase, index],
            recv_sem=recv_sem.at[phase, index],
            device_id={"lon": at_lon(by), "lat": lat + up},
            device_id_type=MESH,
        )

    def slot(by):
        return pl.ds(SLOT[by] * lon_dev, lon_dev)

    def far_slot(by):
        return pl.ds(FAR_SLOT[by] * lon_dev, lon_dev)

    class Phase:
        def __init__(self, phase, source, first, at, buf, far_buf, groups, far_counts, routes):
            self.phase, self.source, self.first, self.at = phase, source, first, at
            self.buf, self.far_buf, self.groups = buf, far_buf, groups
            self.far_counts, self.routes = far_counts, routes

        def rows_of(self, row, count):
            return self.source.at[pl.ds(self.first + row, count), self.at, :]

        def part(self, g, n, by, at):
            row, count = self.groups[g]
            return remote(
                self.phase, g * 4 + n, self.rows_of(row, count),
                self.buf.at[pl.ds(1 + row, count), at, :], by,
            )

        def group(self, g):
            found = [
                self.part(g, 0, side, slot_at(-side)),
                self.part(g, 2, -2 * side, slot_at(2 * side)),
                self.part(g, 3, 2 * side, slot_at(-2 * side)),
            ]
            if self.routes[g] is None:
                found.append(self.part(g, 1, -side, slot_at(side)))
            return found

        def relay(self, g):
            row, count = self.groups[g]
            rows_ = pl.ds(1 + row, count)
            if self.routes[g] == "plane":
                source, target, by = side, -side, 2 * side
            else:
                source, target, by = 2 * side, side, side
            return [
                remote(
                    self.phase, g * 4 + 1, self.buf.at[rows_, slot_at(source), :],
                    self.buf.at[rows_, slot_at(target), :], by,
                )
            ]

        def landed(self, g, which):
            ats = {0: side, 1: -side, 2: 2 * side, 3: -2 * side}
            return [self.part(g, n, side, slot_at(ats[n])) for n in which]

        def pass_on(self, g):
            if self.routes[g]:
                run(self.landed(g, (0,) if self.routes[g] == "plane" else (2,)), "wait_recv")
                run(self.relay(g), "start")

        def arrive(self, g):
            left = {None: (0, 1, 2, 3), "plane": (1, 2, 3), "pair": (0, 1, 3)}
            run(self.landed(g, left[self.routes[g]]), "wait_recv")

        def sent(self, g):
            run(self.group(g), "wait_send")
            if self.routes[g]:
                run(self.relay(g), "wait_send")

        def lift(self, up):
            row, target = (0, rows + 1) if up < 0 else (rows - 1, 0)
            return [
                remote(
                    self.phase, 12 + (0 if up < 0 else 1), self.rows_of(row, 1),
                    self.buf.at[pl.ds(target, 1), own, :], 0, up,
                )
            ]

        def spread(self, up):
            target = rows + 1 if up < 0 else 0
            return [
                remote(
                    self.phase, 14 + n + (0 if up < 0 else 4),
                    self.buf.at[pl.ds(target, 1), own, :],
                    self.buf.at[pl.ds(target, 1), slot(-by), :], by,
                )
                for n, by in enumerate(NEAR)
            ]

        def far(self, pole, reach):
            count = self.far_counts[reach]
            row = 0 if pole == 0 else rows - count
            return [
                remote(
                    self.phase, 22 + FAR.index(by), self.rows_of(row, count),
                    self.far_buf.at[pl.ds(1 + row, count), far_slot(-by), :], by,
                )
                for by in (-reach, reach)
            ]

        def lifts(self, what):
            for up in (-1, 1):
                ok = (above if up < 0 else below) if what != "wait_recv" else (
                    below if up < 0 else above
                )

                @pl.when(ok)
                def _():
                    run(self.lift(up), what)

        def spreads(self, up, what):
            @pl.when(below if up < 0 else above)
            def _():
                run(self.spread(up), what)

        def fars(self, pole, reach, what):
            @pl.when(north if pole == 0 else south)
            def _():
                run(self.far(pole, reach), what)

    def run(copies, what):
        for copy in copies:
            getattr(copy, what)()

    forward = Phase(0, x_hbm, 0, every, xw, xe, ((0, 3), (5, 3), (3, 2)), {3: 5, 4: 3}, ('plane', 'pair', 'plane'))
    backward = Phase(1, gw, 1, own, gw, ge, ((0, 2), (6, 2), (2, 4)), {3: 4, 4: 2}, ('plane', 'pair', None))

    pl.semaphore_wait(
        barrier,
        4 + above.astype(jnp.int32) + below.astype(jnp.int32) + 4 * polar.astype(jnp.int32),
    )
    forward.lifts("start")
    run(forward.group(0), "start")
    run(forward.group(1), "start")
    for pole in (0, 1):
        for reach in (4, 3):
            forward.fars(pole, reach, "start")

    locals_[0].wait()
    line = iota((rows, LANES), 0)
    reach = jnp.zeros((rows, LANES), jnp.int32)
    for i in range(rows):
        reach = jnp.where(line == i, widths[i] * lon_dev, reach)
    keep = jnp.where(
        jnp.abs(iota((rows, LANES), 1) - centre) <= reach,
        lax.rsqrt(3.0 * (2.0 * reach.astype(F32) + 1.0)),
        0.0,
    )
    ff[:, :, :, 256:LANES] = jnp.zeros((kernels, 3, rows, LANES - 256), F32)
    for k in range(kernels):
        for t in range(3):
            ff[k, t, :, 0:taps] = psi[k, t] * keep[:, 0:taps]

    run(forward.group(2), "start")
    forward.lifts("wait_recv")
    for up in (-1, 1):
        forward.spreads(up, "start")
    for g in range(3):
        forward.pass_on(g)

    flip = jnp.where(
        iota((LANES, LANES), 0) + iota((LANES, LANES), 1) == 2 * centre, 1.0, 0.0
    ).astype(BF16)
    flipped = jnp.dot(
        ff[...].reshape(3 * kernels * rows, LANES).astype(BF16), flip, preferred_element_type=F32
    )
    fr[...] = flipped.reshape(kernels, 3, rows, LANES)
    for k in range(kernels):
        fsend[0, k : k + 1, :] = fr[k, 0, 0:1, :]
        fsend[1, k : k + 1, :] = fr[k, 2, rows - 1 : rows, :]

    def filter_copy(up):
        n = 0 if up < 0 else 1
        return remote(0, 26 + n, fsend.at[n], frecv.at[n], 0, up)

    @pl.when(above)
    def _():
        filter_copy(-1).start()

    @pl.when(below)
    def _():
        filter_copy(1).start()

    blank = jnp.zeros((wide, channels), BF16)

    @pl.when(north)
    def _():
        xw[0] = blank
        gw[0] = blank
        frecv[1] = jnp.zeros(frecv.shape[1:], F32)

    @pl.when(south)
    def _():
        xw[rows + 1] = blank
        gw[rows + 1] = blank
        frecv[0] = jnp.zeros(frecv.shape[1:], F32)

    def near_block(base):
        base = jnp.broadcast_to(base, (lon_dev, 256))
        return pltpu.roll(base, 256 - 2 * lon_dev, 1, stride=1, stride_axis=0).astype(BF16)

    def far_block(filters, row, t, k):
        lane = iota((lon_dev, 128), 1)

        def part(first):
            return jnp.broadcast_to(
                filters[k, t, row : row + 1, first : first + 128], (lon_dev, 128)
            )

        low = jnp.where(lane < 2 * lon_dev, part(0), 0.0)
        high = jnp.where(lane > 2 * lon_dev, part(128), part(256))
        low = pltpu.roll(low, 0, 1, stride=1, stride_axis=0)
        high = pltpu.roll(high, 128 - lon_dev, 1, stride=1, stride_axis=0)
        return jnp.where(lane < 2 * lon_dev, low, high).astype(BF16)

    def put(dst, index, k, block):
        dst[index, pl.ds(k * lon_dev, lon_dev), :] = block

    @pl.loop(0, rows)
    def _(i):
        for t in range(3):
            for k in range(kernels):
                put(tf, i * 3 + t, k, near_block(ff[k, t, pl.ds(i, 1), 0:256]))

    locals_[1].wait()
    inside = (iota((channels, channels), 0) // GROUP) == (iota((channels, channels), 1) // GROUP)
    for k in range(kernels):
        four = wg[k].astype(F32)
        eight = jnp.concatenate([four, four], axis=0)
        full = jnp.broadcast_to(eight[None], (channels // 8, 8, channels))
        full = full.reshape(channels, channels)
        wbd[pl.ds(k * channels, channels), :] = jnp.where(inside, full, 0.0).astype(BF16)

    for pole in (0, 1):

        @pl.when(north if pole == 0 else south)
        def _():
            for a in range(4):
                row = a if pole == 0 else rows - 1 - a
                for t in range(3):
                    for k in range(kernels):
                        put(te, a * 3 + t, k, far_block(ff, row, t, k))
                        put(tbe, a * 3 + t, k, far_block(fr, row, t, k))

    @pl.loop(0, rows)
    def _(source):
        for t in range(3):
            for k in range(kernels):
                put(tb, (source + t) * 3 + t, k, near_block(fr[k, t, pl.ds(source, 1), 0:256]))

    @pl.when(below)
    def _():
        filter_copy(-1).wait_recv()

    @pl.when(above)
    def _():
        filter_copy(1).wait_recv()

    for k in range(kernels):
        put(tb, 3 + 2, k, near_block(frecv[1, k : k + 1, 0:256]))
        put(tb, rows * 3, k, near_block(frecv[0, k : k + 1, 0:256]))

    for copy in locals_[2:]:
        copy.wait()

    def far_term(table, index, buf, row, both):
        if both:
            return jnp.dot(table[index], buf[row], preferred_element_type=F32)
        return jnp.dot(
            table[index, :, lon_dev : 3 * lon_dev],
            buf[row, lon_dev : 3 * lon_dev, :],
            preferred_element_type=F32,
        )

    def conv(table, offset, buf, shift, flipped, span):
        first, count = span
        for n in range(count):
            i = first + n
            total = None
            for t in range(3):
                row = i + (2 - t if flipped else t)
                term = jnp.dot(
                    table[(i + offset) * 3 + t, :, 0:wide], buf[row], preferred_element_type=F32
                )
                total = term if total is None else total + term
            acc[n] = total

    def far_conv(table, buf, flipped, span):
        first, count = span
        for pole in (0, 1):
            found = []
            for n in range(count):
                i = first + n
                for t in range(3):
                    source = i + (1 - t if flipped else t - 1)
                    away = source if pole == 0 else rows - 1 - source
                    a = i if pole == 0 else rows - 1 - i
                    filter_row = away if flipped else a
                    if 0 <= filter_row < 4 and away >= 0:
                        found.append((n, filter_row, t, source))
            if not found:
                continue

            @pl.when(north if pole == 0 else south)
            def _():
                for n, a, t, source in found:
                    acc[n] += far_term(table, a * 3 + t, buf, source + 1, a < 2)

    def gather(span):
        for n in range(span[1]):
            for k in range(kernels):
                cv[pl.ds(n * lon_dev, lon_dev), pl.ds(k * channels, channels)] = acc[
                    n, pl.ds(k * lon_dev, lon_dev), :
                ].astype(BF16)
        return pl.ds(0, span[1] * lon_dev)

    root = 0.7978845608028654
    cubic = 0.044715

    def forward_rows(span):
        first, count = span
        conv(tf, 0, xw, 0, False, span)
        far_conv(te, xe, False, span)
        at = gather(span)
        mixed = jnp.dot(cv[at, :], wbd[...], preferred_element_type=F32).astype(BF16)
        v = jnp.dot(mixed, wm[...], preferred_element_type=F32)
        square = v * v
        th = jnp.tanh(root * v * (1.0 + cubic * square))
        half = 0.5 * (1.0 + th)
        mine = pl.ds(first, count)
        shape = (count, lon_dev, channels)
        slope = half + 0.5 * v * (1.0 - th * th) * (root * (1.0 + 3.0 * cubic * square))
        pulled = go[mine].astype(F32).reshape(count * lon_dev, channels) * slope
        back = lax.dot_general(
            pulled.astype(BF16), wm[...], (((1,), (1,)), ((), ())), preferred_element_type=F32
        )
        gw[pl.ds(1 + first, count), own, :] = back.astype(BF16).reshape(shape)
        out_ref[mine] = (v * half).astype(BF16).reshape(shape)

    def backward_rows(span):
        first, count = span
        conv(tb, 1, gw, 0, True, span)
        far_conv(tbe, ge, True, span)
        at = gather(span)
        total = None
        for k in range(kernels):
            lanes = pl.ds(k * channels, channels)
            term = lax.dot_general(
                cv[at, lanes], wbd[lanes, :], (((1,), (1,)), ((), ())), preferred_element_type=F32
            )
            total = term if total is None else total + term
        gin_ref[pl.ds(first, count)] = total.astype(BF16).reshape(count, lon_dev, channels)

    forward.arrive(0)
    forward.spreads(1, "wait_recv")
    for reach in (4, 3):
        for pole in (0, 1):
            forward.fars(pole, reach, "wait_recv")
    forward_rows((0, 2))
    run(backward.group(0), "start")

    @pl.when(above)
    def _():
        run(backward.lift(-1), "start")

    backward.fars(0, 4, "start")
    forward.arrive(1)
    forward.spreads(-1, "wait_recv")
    forward_rows((6, 2))
    run(backward.group(1), "start")

    @pl.when(below)
    def _():
        run(backward.lift(1), "start")

    backward.fars(1, 4, "start")
    forward.arrive(2)
    forward_rows((2, 4))
    run(backward.group(2), "start")
    for pole in (0, 1):
        backward.fars(pole, 3, "start")
    backward.pass_on(0)
    backward.pass_on(1)
    backward.lifts("wait_recv")
    for up in (-1, 1):
        backward.spreads(up, "start")
    backward.pass_on(2)

    for g in range(3):
        backward.arrive(g)
    for reach in (4, 3):
        for pole in (0, 1):
            backward.fars(pole, reach, "wait_recv")
    backward_rows((2, 4))
    backward.spreads(1, "wait_recv")
    backward_rows((0, 2))
    backward.spreads(-1, "wait_recv")
    backward_rows((6, 2))

    for phase in (forward, backward):
        for g in range(3):
            phase.sent(g)
        phase.lifts("wait_send")
        for up in (-1, 1):
            phase.spreads(up, "wait_send")
        for pole in (0, 1):
            for reach in (4, 3):
                phase.fars(pole, reach, "wait_send")

    @pl.when(above)
    def _():
        filter_copy(-1).wait_send()

    @pl.when(below)
    def _():
        filter_copy(1).wait_send()


def body(n_lon, n_lat, inputs, psi_raw, widths, w_group, w_mix, grad_out):
    rows, lon_dev, channels = inputs.shape
    kernels = psi_raw.shape[0]
    wide = 5 * lon_dev
    depth = kernels * lon_dev
    copies = 28
    psi_raw = jnp.transpose(psi_raw, (0, 2, 1, 3))
    anywhere = pl.BlockSpec(memory_space=pltpu.HBM)
    vmem = pl.BlockSpec(memory_space=pltpu.VMEM)
    shape = jax.ShapeDtypeStruct(inputs.shape, BF16)
    return pl.pallas_call(
        functools.partial(kernel, n_lon, n_lat),
        name="disco",
        out_shape=(pltpu.VMEM(inputs.shape, BF16), pltpu.VMEM(inputs.shape, BF16)),
        in_specs=[
            anywhere, anywhere, pl.BlockSpec(memory_space=pltpu.SMEM),
            anywhere, anywhere, anywhere,
        ],
        out_specs=(vmem, vmem),
        scratch_shapes=[
            pltpu.VMEM(psi_raw.shape, F32),
            pltpu.VMEM(w_group.shape, BF16),
            pltpu.VMEM(w_mix.shape, BF16),
            pltpu.VMEM(grad_out.shape, BF16),
            pltpu.VMEM((rows + 2, wide, channels), BF16),
            pltpu.VMEM((rows + 2, wide, channels), BF16),
            pltpu.VMEM((rows + 2, 4 * lon_dev, channels), BF16),
            pltpu.VMEM((rows + 2, 4 * lon_dev, channels), BF16),
            pltpu.VMEM((kernels, 3, rows, LANES), F32),
            pltpu.VMEM((kernels, 3, rows, LANES), F32),
            pltpu.VMEM((2, 8, LANES), F32),
            pltpu.VMEM((2, 8, LANES), F32),
            pltpu.VMEM((rows * 3, depth, 256), BF16),
            pltpu.VMEM(((rows + 2) * 3, depth, 256), BF16),
            pltpu.VMEM((12, depth, 4 * lon_dev), BF16),
            pltpu.VMEM((12, depth, 4 * lon_dev), BF16),
            pltpu.VMEM((kernels * channels, channels), BF16),
            pltpu.VMEM((4 * lon_dev, kernels * channels), BF16),
            pltpu.VMEM((4, depth, channels), F32),
            pltpu.SemaphoreType.DMA((5,)),
            pltpu.SemaphoreType.DMA((2, copies)),
            pltpu.SemaphoreType.DMA((2, copies)),
        ],
        compiler_params=pltpu.CompilerParams(
            collective_id=0, has_side_effects=True
        ),
        cost_estimate=pl.CostEstimate(
            flops=4_000_000_000, bytes_accessed=2_000_000, transcendentals=65536
        ),
    )(inputs, psi_raw, widths, w_group, w_mix, grad_out)


def solution(mesh):
    return jax.shard_map(
        functools.partial(body, mesh.shape["lon"], mesh.shape["lat"]),
        mesh=mesh,
        in_specs=(
            P("lat", "lon", None),
            P(None, "lat", None, None),
            P("lat"),
            P(),
            P(),
            P("lat", "lon", None),
        ),
        out_specs=(P("lat", "lon", None), P("lat", "lon", None)),
        check_vma=False,
    )
```

```python
import functools

import jax
import jax.numpy as jnp
from jax import lax
from jax.experimental import pallas as pl
from jax.experimental.pallas import tpu as pltpu
from jax.sharding import PartitionSpec as P

GROUP = 4
SMAX = 4
LANES = 384
NEAR = (-1, 1, -2, 2)
SLOT = {-2: 0, -1: 1, 0: 2, 1: 3, 2: 4}
FAR_SLOT = {-4: 0, -3: 1, 3: 2, 4: 3}
MESH = pl.DeviceIdType.MESH
F32 = jnp.float32
BF16 = jnp.bfloat16


def iota(shape, axis):
    return lax.broadcasted_iota(jnp.int32, shape, axis)


def kernel(
    n_lon, n_lat,
    x_hbm, psi_hbm, widths, wg_hbm, wm_hbm, go_hbm,
    out_ref, gin_ref,
    psi, wg, wm, go, xw, gw, xe, ge, ff, fr, fsend, frecv, tf, tb, te, tbe, wbd, cv, acc,
    local_sem, send_sem, recv_sem,
):
    rows, lon_dev, channels = x_hbm.shape
    kernels, taps = psi_hbm.shape[0], psi_hbm.shape[3]
    centre = SMAX * lon_dev
    wide = lon_dev * 5
    lon, lat = lax.axis_index("lon"), lax.axis_index("lat")
    north, south = lat == 0, lat == n_lat - 1
    above, below = jnp.logical_not(north), jnp.logical_not(south)

    def at_lon(by):
        return lax.rem(lon + (by + n_lon), n_lon)

    barrier = pltpu.get_barrier_semaphore()

    def greet(by, up):
        pl.semaphore_signal(
            barrier, inc=1, device_id={"lon": at_lon(by), "lat": lat + up}, device_id_type=MESH
        )

    for by in NEAR:
        greet(by, 0)

    @pl.when(above)
    def _():
        greet(0, -1)

    @pl.when(below)
    def _():
        greet(0, 1)

    polar = jnp.logical_or(north, south)

    @pl.when(polar)
    def _():
        for by in (-3, 3):
            greet(by, 0)

    own = pl.ds(SLOT[0] * lon_dev, lon_dev)
    every = pl.ds(0, lon_dev)
    locals_ = [
        pltpu.make_async_copy(psi_hbm, psi, local_sem.at[0]),
        pltpu.make_async_copy(wg_hbm, wg, local_sem.at[1]),
        pltpu.make_async_copy(wm_hbm, wm, local_sem.at[2]),
        pltpu.make_async_copy(go_hbm, go, local_sem.at[3]),
        pltpu.make_async_copy(x_hbm, xw.at[pl.ds(1, rows), own, :], local_sem.at[4]),
    ]
    for copy in locals_:
        copy.start()

    side = 1 - 2 * lax.rem(lon, 2)

    def slot_at(by):
        return pl.ds(pl.multiple_of((by + 2) * lon_dev, lon_dev), lon_dev)

    def remote(phase, index, src, dst, by, up=0):
        return pltpu.make_async_remote_copy(
            src_ref=src,
            dst_ref=dst,
            send_sem=send_sem.at[phase, index],
            recv_sem=recv_sem.at[phase, index],
            device_id={"lon": at_lon(by), "lat": lat + up},
            device_id_type=MESH,
        )

    def slot(by):
        return pl.ds(SLOT[by] * lon_dev, lon_dev)

    def far_slot(by):
        return pl.ds(FAR_SLOT[by] * lon_dev, lon_dev)

    class Phase:
        def __init__(self, phase, source, first, at, buf, far_buf, groups, far_count, routes, diagonal):
            self.phase, self.source, self.first, self.at = phase, source, first, at
            self.buf, self.far_buf, self.groups = buf, far_buf, groups
            self.far_count, self.routes, self.diagonal = far_count, routes, diagonal

        def rows_of(self, row, count):
            return self.source.at[pl.ds(self.first + row, count), self.at, :]

        def part(self, g, n, by, at):
            row, count = self.groups[g]
            return remote(
                self.phase, g * 4 + n, self.rows_of(row, count),
                self.buf.at[pl.ds(1 + row, count), at, :], by,
            )

        def group(self, g):
            found = [
                self.part(g, 0, side, slot_at(-side)),
                self.part(g, 2, -2 * side, slot_at(2 * side)),
                self.part(g, 3, 2 * side, slot_at(-2 * side)),
            ]
            if self.routes[g] is None:
                found.append(self.part(g, 1, -side, slot_at(side)))
            return found

        def relay(self, g):
            row, count = self.groups[g]
            rows_ = pl.ds(1 + row, count)
            if self.routes[g] == "plane":
                source, target, by = side, -side, 2 * side
            else:
                source, target, by = 2 * side, side, side
            return [
                remote(
                    self.phase, g * 4 + 1, self.buf.at[rows_, slot_at(source), :],
                    self.buf.at[rows_, slot_at(target), :], by,
                )
            ]

        def landed(self, g, which):
            ats = {0: side, 1: -side, 2: 2 * side, 3: -2 * side}
            return [self.part(g, n, side, slot_at(ats[n])) for n in which]

        def pass_on(self, g):
            run(self.landed(g, (0, 2, 3)), "wait_recv")
            if self.routes[g]:
                run(self.relay(g), "start")

        def arrive(self, g):
            run(self.landed(g, (1,)), "wait_recv")

        def sent(self, g):
            run(self.group(g), "wait_send")
            if self.routes[g]:
                run(self.relay(g), "wait_send")

        def lift(self, up):
            row, target = (0, rows + 1) if up < 0 else (rows - 1, 0)
            target = pl.ds(target, 1)
            found = [
                remote(
                    self.phase, 12 + (0 if up < 0 else 1), self.rows_of(row, 1),
                    self.buf.at[target, own, :], 0, up,
                )
            ]
            if self.diagonal:
                found += [
                    remote(
                        self.phase, 14 + n + (0 if up < 0 else 4), self.rows_of(row, 1),
                        self.buf.at[target, slot(-by), :], by, up,
                    )
                    for n, by in enumerate(NEAR)
                ]
            return found

        def spread(self, up):
            target = rows + 1 if up < 0 else 0
            if self.diagonal:
                return []
            return [
                remote(
                    self.phase, 14 + n + (0 if up < 0 else 4),
                    self.buf.at[pl.ds(target, 1), own, :],
                    self.buf.at[pl.ds(target, 1), slot(-by), :], by,
                )
                for n, by in enumerate(NEAR)
            ]

        def far(self, pole, early):
            count = self.far_count
            if early:
                rows_ = pl.ds(1 if pole == 0 else 1 + rows - count, count)
                return [
                    remote(
                        self.phase, 22 + 2 * (reach - 3) + (s + 1) // 2,
                        self.buf.at[rows_, slot(2 * s), :],
                        self.far_buf.at[rows_, far_slot(s * reach), :], -s * (reach - 2),
                    )
                    for reach in (3, 4)
                    for s in (-1, 1)
                ]
            row = count if pole == 0 else rows - count - 2
            return [
                remote(
                    self.phase, 28 + (s + 1) // 2, self.rows_of(row, 2),
                    self.far_buf.at[pl.ds(1 + row, 2), far_slot(-3 * s), :], 3 * s,
                )
                for s in (-1, 1)
            ]

        def lifts(self, what):
            for up in (-1, 1):
                ok = (above if up < 0 else below) if what != "wait_recv" else (
                    below if up < 0 else above
                )

                @pl.when(ok)
                def _():
                    run(self.lift(up), what)

        def spreads(self, up, what):
            @pl.when(below if up < 0 else above)
            def _():
                run(self.spread(up), what)

        def fars(self, pole, early, what):
            @pl.when(north if pole == 0 else south)
            def _():
                run(self.far(pole, early), what)

    def run(copies, what):
        for copy in copies:
            getattr(copy, what)()

    forward = Phase(0, x_hbm, 0, every, xw, xe, ((0, 3), (5, 3), (3, 2)), 3, ('plane', 'pair', 'plane'), False)
    backward = Phase(1, gw, 1, own, gw, ge, ((0, 2), (6, 2), (2, 4)), 2, ('plane', 'pair', None), True)

    pl.semaphore_wait(
        barrier,
        4 + above.astype(jnp.int32) + below.astype(jnp.int32) + 2 * polar.astype(jnp.int32),
    )
    forward.lifts("start")
    run(forward.group(0), "start")
    run(forward.group(1), "start")
    for pole in (0, 1):
        forward.fars(pole, False, "start")
    run(forward.group(2), "start")

    locals_[0].wait()
    line = iota((rows, LANES), 0)
    reach = jnp.zeros((rows, LANES), jnp.int32)
    for i in range(rows):
        reach = jnp.where(line == i, widths[i] * lon_dev, reach)
    keep = jnp.where(
        jnp.abs(iota((rows, LANES), 1) - centre) <= reach,
        lax.rsqrt(3.0 * (2.0 * reach.astype(F32) + 1.0)),
        0.0,
    )
    ff[:, :, :, 256:LANES] = jnp.zeros((kernels, 3, rows, LANES - 256), F32)
    for k in range(kernels):
        for t in range(3):
            ff[k, t, :, 0:taps] = psi[k, t] * keep[:, 0:taps]


    flip = jnp.where(
        iota((LANES, LANES), 0) + iota((LANES, LANES), 1) == 2 * centre, 1.0, 0.0
    ).astype(BF16)
    flipped = jnp.dot(
        ff[...].reshape(3 * kernels * rows, LANES).astype(BF16), flip, preferred_element_type=F32
    )
    fr[...] = flipped.reshape(kernels, 3, rows, LANES)
    for k in range(kernels):
        fsend[0, k : k + 1, :] = fr[k, 0, 0:1, :]
        fsend[1, k : k + 1, :] = fr[k, 2, rows - 1 : rows, :]

    def filter_copy(up):
        n = 0 if up < 0 else 1
        return remote(0, 26 + n, fsend.at[n], frecv.at[n], 0, up)

    @pl.when(above)
    def _():
        filter_copy(-1).start()

    @pl.when(below)
    def _():
        filter_copy(1).start()

    blank = jnp.zeros((wide, channels), BF16)

    @pl.when(north)
    def _():
        xw[0] = blank
        gw[0] = blank
        frecv[1] = jnp.zeros(frecv.shape[1:], F32)

    @pl.when(south)
    def _():
        xw[rows + 1] = blank
        gw[rows + 1] = blank
        frecv[0] = jnp.zeros(frecv.shape[1:], F32)

    def near_block(base):
        base = jnp.broadcast_to(base, (lon_dev, 256))
        return pltpu.roll(base, 256 - 2 * lon_dev, 1, stride=1, stride_axis=0).astype(BF16)

    def far_block(filters, row, t, k):
        lane = iota((lon_dev, 128), 1)

        def part(first):
            return jnp.broadcast_to(
                filters[k, t, row : row + 1, first : first + 128], (lon_dev, 128)
            )

        low = jnp.where(lane < 2 * lon_dev, part(0), 0.0)
        high = jnp.where(lane > 2 * lon_dev, part(128), part(256))
        low = pltpu.roll(low, 0, 1, stride=1, stride_axis=0)
        high = pltpu.roll(high, 128 - lon_dev, 1, stride=1, stride_axis=0)
        return jnp.where(lane < 2 * lon_dev, low, high).astype(BF16)

    def put(dst, index, k, block):
        dst[index, pl.ds(k * lon_dev, lon_dev), :] = block

    @pl.loop(0, rows)
    def _(i):
        for t in range(3):
            for k in range(kernels):
                put(tf, i * 3 + t, k, near_block(ff[k, t, pl.ds(i, 1), 0:256]))

    forward.lifts("wait_recv")
    for up in (-1, 1):
        forward.spreads(up, "start")
    forward.pass_on(0)
    forward.fars(0, True, "start")
    forward.pass_on(1)
    forward.fars(1, True, "start")

    locals_[1].wait()
    inside = (iota((channels, channels), 0) // GROUP) == (iota((channels, channels), 1) // GROUP)
    for k in range(kernels):
        four = wg[k].astype(F32)
        eight = jnp.concatenate([four, four], axis=0)
        full = jnp.broadcast_to(eight[None], (channels // 8, 8, channels))
        full = full.reshape(channels, channels)
        wbd[pl.ds(k * channels, channels), :] = jnp.where(inside, full, 0.0).astype(BF16)

    @pl.loop(0, rows)
    def _(source):
        for t in range(3):
            for k in range(kernels):
                put(tb, (source + t) * 3 + t, k, near_block(fr[k, t, pl.ds(source, 1), 0:256]))

    forward.pass_on(2)
    for pole in (0, 1):

        @pl.when(north if pole == 0 else south)
        def _():
            for a in range(4):
                row = a if pole == 0 else rows - 1 - a
                for t in range(3):
                    for k in range(kernels):
                        put(te, a * 3 + t, k, far_block(ff, row, t, k))
                        put(tbe, a * 3 + t, k, far_block(fr, row, t, k))

    @pl.when(below)
    def _():
        filter_copy(-1).wait_recv()

    @pl.when(above)
    def _():
        filter_copy(1).wait_recv()

    for k in range(kernels):
        put(tb, 3 + 2, k, near_block(frecv[1, k : k + 1, 0:256]))
        put(tb, rows * 3, k, near_block(frecv[0, k : k + 1, 0:256]))

    for copy in locals_[2:]:
        copy.wait()

    def far_term(table, index, buf, row, both):
        if both:
            return jnp.dot(table[index], buf[row], preferred_element_type=F32)
        return jnp.dot(
            table[index, :, lon_dev : 3 * lon_dev],
            buf[row, lon_dev : 3 * lon_dev, :],
            preferred_element_type=F32,
        )

    def conv(table, offset, buf, shift, flipped, span):
        first, count = span
        for n in range(count):
            i = first + n
            total = None
            for t in range(3):
                row = i + (2 - t if flipped else t)
                term = jnp.dot(
                    table[(i + offset) * 3 + t, :, 0:wide], buf[row], preferred_element_type=F32
                )
                total = term if total is None else total + term
            acc[n] = total

    def far_conv(table, buf, flipped, span):
        first, count = span
        for pole in (0, 1):
            found = []
            for n in range(count):
                i = first + n
                for t in range(3):
                    source = i + (1 - t if flipped else t - 1)
                    away = source if pole == 0 else rows - 1 - source
                    a = i if pole == 0 else rows - 1 - i
                    filter_row = away if flipped else a
                    if 0 <= filter_row < 4 and away >= 0:
                        found.append((n, filter_row, t, source))
            if not found:
                continue

            @pl.when(north if pole == 0 else south)
            def _():
                for n, a, t, source in found:
                    acc[n] += far_term(table, a * 3 + t, buf, source + 1, a < 2)

    def gather(span):
        for n in range(span[1]):
            for k in range(kernels):
                cv[pl.ds(n * lon_dev, lon_dev), pl.ds(k * channels, channels)] = acc[
                    n, pl.ds(k * lon_dev, lon_dev), :
                ].astype(BF16)
        return pl.ds(0, span[1] * lon_dev)

    root = 0.7978845608028654
    cubic = 0.044715

    def forward_rows(span):
        first, count = span
        conv(tf, 0, xw, 0, False, span)
        far_conv(te, xe, False, span)
        at = gather(span)
        mixed = jnp.dot(cv[at, :], wbd[...], preferred_element_type=F32).astype(BF16)
        v = jnp.dot(mixed, wm[...], preferred_element_type=F32)
        square = v * v
        th = jnp.tanh(root * v * (1.0 + cubic * square))
        half = 0.5 * (1.0 + th)
        mine = pl.ds(first, count)
        shape = (count, lon_dev, channels)
        slope = half + 0.5 * v * (1.0 - th * th) * (root * (1.0 + 3.0 * cubic * square))
        pulled = go[mine].astype(F32).reshape(count * lon_dev, channels) * slope
        back = lax.dot_general(
            pulled.astype(BF16), wm[...], (((1,), (1,)), ((), ())), preferred_element_type=F32
        )
        gw[pl.ds(1 + first, count), own, :] = back.astype(BF16).reshape(shape)
        out_ref[mine] = (v * half).astype(BF16).reshape(shape)

    def backward_rows(span):
        first, count = span
        conv(tb, 1, gw, 0, True, span)
        far_conv(tbe, ge, True, span)
        at = gather(span)
        total = None
        for k in range(kernels):
            lanes = pl.ds(k * channels, channels)
            term = lax.dot_general(
                cv[at, lanes], wbd[lanes, :], (((1,), (1,)), ((), ())), preferred_element_type=F32
            )
            total = term if total is None else total + term
        gin_ref[pl.ds(first, count)] = total.astype(BF16).reshape(count, lon_dev, channels)

    forward.arrive(0)
    forward.spreads(1, "wait_recv")
    forward.fars(0, True, "wait_recv")
    forward_rows((0, 2))
    run(backward.group(0), "start")

    @pl.when(above)
    def _():
        run(backward.lift(-1), "start")

    forward.arrive(1)
    forward.spreads(-1, "wait_recv")
    forward.fars(1, True, "wait_recv")
    forward_rows((6, 2))
    run(backward.group(1), "start")

    @pl.when(below)
    def _():
        run(backward.lift(1), "start")

    forward.arrive(2)
    for pole in (0, 1):
        forward.fars(pole, False, "wait_recv")
    forward_rows((2, 4))
    for pole in (0, 1):
        backward.fars(pole, False, "start")
    run(backward.group(2), "start")
    backward.lifts("wait_recv")
    for up in (-1, 1):
        backward.spreads(up, "start")
    backward.pass_on(0)
    backward.fars(0, True, "start")
    backward.pass_on(1)
    backward.fars(1, True, "start")
    backward.pass_on(2)

    for g in range(3):
        backward.arrive(g)
    for early in (True, False):
        for pole in (0, 1):
            backward.fars(pole, early, "wait_recv")
    backward_rows((2, 4))
    backward.spreads(1, "wait_recv")
    backward_rows((0, 2))
    backward.spreads(-1, "wait_recv")
    backward_rows((6, 2))

    for phase in (forward, backward):
        for g in range(3):
            phase.sent(g)
        phase.lifts("wait_send")
        for up in (-1, 1):
            phase.spreads(up, "wait_send")
        for pole in (0, 1):
            for early in (True, False):
                phase.fars(pole, early, "wait_send")

    @pl.when(above)
    def _():
        filter_copy(-1).wait_send()

    @pl.when(below)
    def _():
        filter_copy(1).wait_send()


def body(n_lon, n_lat, inputs, psi_raw, widths, w_group, w_mix, grad_out):
    rows, lon_dev, channels = inputs.shape
    kernels = psi_raw.shape[0]
    wide = 5 * lon_dev
    depth = kernels * lon_dev
    copies = 30
    psi_raw = jnp.transpose(psi_raw, (0, 2, 1, 3))
    anywhere = pl.BlockSpec(memory_space=pltpu.HBM)
    vmem = pl.BlockSpec(memory_space=pltpu.VMEM)
    shape = jax.ShapeDtypeStruct(inputs.shape, BF16)
    return pl.pallas_call(
        functools.partial(kernel, n_lon, n_lat),
        name="disco",
        out_shape=(pltpu.VMEM(inputs.shape, BF16), pltpu.VMEM(inputs.shape, BF16)),
        in_specs=[
            anywhere, anywhere, pl.BlockSpec(memory_space=pltpu.SMEM),
            anywhere, anywhere, anywhere,
        ],
        out_specs=(vmem, vmem),
        scratch_shapes=[
            pltpu.VMEM(psi_raw.shape, F32),
            pltpu.VMEM(w_group.shape, BF16),
            pltpu.VMEM(w_mix.shape, BF16),
            pltpu.VMEM(grad_out.shape, BF16),
            pltpu.VMEM((rows + 2, wide, channels), BF16),
            pltpu.VMEM((rows + 2, wide, channels), BF16),
            pltpu.VMEM((rows + 2, 4 * lon_dev, channels), BF16),
            pltpu.VMEM((rows + 2, 4 * lon_dev, channels), BF16),
            pltpu.VMEM((kernels, 3, rows, LANES), F32),
            pltpu.VMEM((kernels, 3, rows, LANES), F32),
            pltpu.VMEM((2, 8, LANES), F32),
            pltpu.VMEM((2, 8, LANES), F32),
            pltpu.VMEM((rows * 3, depth, 256), BF16),
            pltpu.VMEM(((rows + 2) * 3, depth, 256), BF16),
            pltpu.VMEM((12, depth, 4 * lon_dev), BF16),
            pltpu.VMEM((12, depth, 4 * lon_dev), BF16),
            pltpu.VMEM((kernels * channels, channels), BF16),
            pltpu.VMEM((4 * lon_dev, kernels * channels), BF16),
            pltpu.VMEM((4, depth, channels), F32),
            pltpu.SemaphoreType.DMA((5,)),
            pltpu.SemaphoreType.DMA((2, copies)),
            pltpu.SemaphoreType.DMA((2, copies)),
        ],
        compiler_params=pltpu.CompilerParams(
            collective_id=0, has_side_effects=True
        ),
        cost_estimate=pl.CostEstimate(
            flops=4_000_000_000, bytes_accessed=2_000_000, transcendentals=65536
        ),
    )(inputs, psi_raw, widths, w_group, w_mix, grad_out)


def solution(mesh):
    return jax.shard_map(
        functools.partial(body, mesh.shape["lon"], mesh.shape["lat"]),
        mesh=mesh,
        in_specs=(
            P("lat", "lon", None),
            P(None, "lat", None, None),
            P("lat"),
            P(),
            P(),
            P("lat", "lon", None),
        ),
        out_specs=(P("lat", "lon", None), P("lat", "lon", None)),
        check_vma=False,
    )
```

```python
import functools

import jax
import jax.numpy as jnp
from jax import lax
from jax.experimental import pallas as pl
from jax.experimental.pallas import tpu as pltpu
from jax.sharding import PartitionSpec as P

GROUP = 4
SMAX = 4
LANES = 384
NEAR = (-1, 1, -2, 2)
SLOT = {-2: 0, -1: 1, 0: 2, 1: 3, 2: 4}
FAR_SLOT = {-4: 0, -3: 1, 3: 2, 4: 3}
MESH = pl.DeviceIdType.MESH
F32 = jnp.float32
BF16 = jnp.bfloat16


def iota(shape, axis):
    return lax.broadcasted_iota(jnp.int32, shape, axis)


def kernel(
    n_lon, n_lat,
    x_hbm, psi_hbm, widths, wg_hbm, wm_hbm, go_hbm,
    both_ref,
    psi, wg, wm, go, xw, gw, xe, ge, ff, fr, fsend, frecv, tf, tb, te, tbe, wbd, cv, acc,
    local_sem, send_sem, recv_sem,
):
    out_ref, gin_ref = both_ref.at[0], both_ref.at[1]
    rows, lon_dev, channels = x_hbm.shape
    kernels, taps = psi_hbm.shape[0], psi_hbm.shape[3]
    centre = SMAX * lon_dev
    wide = lon_dev * 5
    lon, lat = lax.axis_index("lon"), lax.axis_index("lat")
    north, south = lat == 0, lat == n_lat - 1
    above, below = jnp.logical_not(north), jnp.logical_not(south)

    def at_lon(by):
        return lax.rem(lon + (by + n_lon), n_lon)

    barrier = pltpu.get_barrier_semaphore()

    def greet(by, up):
        pl.semaphore_signal(
            barrier, inc=1, device_id={"lon": at_lon(by), "lat": lat + up}, device_id_type=MESH
        )

    for by in NEAR:
        greet(by, 0)

    @pl.when(above)
    def _():
        greet(0, -1)

    @pl.when(below)
    def _():
        greet(0, 1)

    polar = jnp.logical_or(north, south)

    @pl.when(polar)
    def _():
        for by in (-3, 3):
            greet(by, 0)

    own = pl.ds(SLOT[0] * lon_dev, lon_dev)
    every = pl.ds(0, lon_dev)
    locals_ = [
        pltpu.make_async_copy(psi_hbm, psi, local_sem.at[0]),
        pltpu.make_async_copy(wg_hbm, wg, local_sem.at[1]),
        pltpu.make_async_copy(wm_hbm, wm, local_sem.at[2]),
        pltpu.make_async_copy(go_hbm, go, local_sem.at[3]),
        pltpu.make_async_copy(x_hbm, xw.at[pl.ds(1, rows), own, :], local_sem.at[4]),
    ]
    for copy in locals_:
        copy.start()

    side = 1 - 2 * lax.rem(lon, 2)

    def slot_at(by):
        return pl.ds(pl.multiple_of((by + 2) * lon_dev, lon_dev), lon_dev)

    def remote(phase, index, src, dst, by, up=0):
        return pltpu.make_async_remote_copy(
            src_ref=src,
            dst_ref=dst,
            send_sem=send_sem.at[phase, index],
            recv_sem=recv_sem.at[phase, index],
            device_id={"lon": at_lon(by), "lat": lat + up},
            device_id_type=MESH,
        )

    def slot(by):
        return pl.ds(SLOT[by] * lon_dev, lon_dev)

    def far_slot(by):
        return pl.ds(FAR_SLOT[by] * lon_dev, lon_dev)

    class Phase:
        def __init__(self, phase, source, first, at, buf, far_buf, groups, far_count, routes):
            self.phase, self.source, self.first, self.at = phase, source, first, at
            self.buf, self.far_buf, self.groups = buf, far_buf, groups
            self.far_count, self.routes = far_count, routes

        def first_of(self, g):
            row, count = self.groups[g]
            return jnp.where(south, rows - row - count, row)

        def rows_of(self, row, count):
            return self.source.at[pl.ds(self.first + row, count), self.at, :]

        def part(self, g, n, by, at):
            row, count = self.first_of(g), self.groups[g][1]
            return remote(
                self.phase, g * 4 + n, self.rows_of(row, count),
                self.buf.at[pl.ds(1 + row, count), at, :], by,
            )

        def group(self, g):
            found = [
                self.part(g, 0, side, slot_at(-side)),
                self.part(g, 2, -2 * side, slot_at(2 * side)),
                self.part(g, 3, 2 * side, slot_at(-2 * side)),
            ]
            if self.routes[g] is None:
                found.append(self.part(g, 1, -side, slot_at(side)))
            return found

        def relay(self, g):
            rows_ = pl.ds(1 + self.first_of(g), self.groups[g][1])
            if self.routes[g] == "plane":
                source, target, by = side, -side, 2 * side
            else:
                source, target, by = 2 * side, side, side
            return [
                remote(
                    self.phase, g * 4 + 1, self.buf.at[rows_, slot_at(source), :],
                    self.buf.at[rows_, slot_at(target), :], by,
                )
            ]

        def landed(self, g, which):
            ats = {0: side, 1: -side, 2: 2 * side, 3: -2 * side}
            return [self.part(g, n, side, slot_at(ats[n])) for n in which]

        def pass_on(self, g):
            run(self.landed(g, (0, 2, 3)), "wait_recv")
            if self.routes[g]:
                run(self.relay(g), "start")

        def arrive(self, g):
            run(self.landed(g, (1,)), "wait_recv")

        def sent(self, g):
            run(self.group(g), "wait_send")
            if self.routes[g]:
                run(self.relay(g), "wait_send")

        def lift(self, up):
            row, target = (0, rows + 1) if up < 0 else (rows - 1, 0)
            return [
                remote(
                    self.phase, 12 + (0 if up < 0 else 1), self.rows_of(row, 1),
                    self.buf.at[pl.ds(target, 1), own, :], 0, up,
                )
            ]

        def spread(self, up):
            target = rows + 1 if up < 0 else 0
            return [
                remote(
                    self.phase, 14 + n + (0 if up < 0 else 4),
                    self.buf.at[pl.ds(target, 1), own, :],
                    self.buf.at[pl.ds(target, 1), slot(-by), :], by,
                )
                for n, by in enumerate(NEAR)
            ]

        def far(self, pole, early):
            count = self.far_count
            if early:
                rows_ = pl.ds(1 if pole == 0 else 1 + rows - count, count)
                return [
                    remote(
                        self.phase, 22 + 2 * (reach - 3) + (s + 1) // 2,
                        self.buf.at[rows_, slot(2 * s), :],
                        self.far_buf.at[rows_, far_slot(s * reach), :], -s * (reach - 2),
                    )
                    for reach in (3, 4)
                    for s in (-1, 1)
                ]
            row = count if pole == 0 else rows - count - 2
            return [
                remote(
                    self.phase, 28 + (s + 1) // 2, self.rows_of(row, 2),
                    self.far_buf.at[pl.ds(1 + row, 2), far_slot(-3 * s), :], 3 * s,
                )
                for s in (-1, 1)
            ]

        def lifts(self, what):
            for up in (-1, 1):
                ok = (above if up < 0 else below) if what != "wait_recv" else (
                    below if up < 0 else above
                )

                @pl.when(ok)
                def _():
                    run(self.lift(up), what)

        def spreads(self, up, what):
            @pl.when(below if up < 0 else above)
            def _():
                run(self.spread(up), what)

        def fars(self, pole, early, what):
            @pl.when(north if pole == 0 else south)
            def _():
                run(self.far(pole, early), what)

    def run(copies, what):
        for copy in copies:
            getattr(copy, what)()

    forward = Phase(0, x_hbm, 0, every, xw, xe, ((0, 3), (5, 3), (3, 2)), 3, ('pair', 'plane', 'pair'))
    backward = Phase(1, gw, 1, own, gw, ge, ((0, 2), (6, 2), (2, 4)), 2, ('pair', 'plane', None))

    pl.semaphore_wait(
        barrier,
        4 + above.astype(jnp.int32) + below.astype(jnp.int32) + 2 * polar.astype(jnp.int32),
    )
    forward.lifts("start")
    run(forward.group(0), "start")
    run(forward.group(1), "start")
    for pole in (0, 1):
        forward.fars(pole, False, "start")
    run(forward.group(2), "start")

    locals_[0].wait()
    line = iota((rows, LANES), 0)
    reach = jnp.zeros((rows, LANES), jnp.int32)
    for i in range(rows):
        reach = jnp.where(line == i, widths[i] * lon_dev, reach)
    keep = jnp.where(
        jnp.abs(iota((rows, LANES), 1) - centre) <= reach,
        lax.rsqrt(3.0 * (2.0 * reach.astype(F32) + 1.0)),
        0.0,
    )
    ff[:, :, :, 256:LANES] = jnp.zeros((kernels, 3, rows, LANES - 256), F32)
    for k in range(kernels):
        for t in range(3):
            ff[k, t, :, 0:taps] = psi[k, t] * keep[:, 0:taps]


    flip = jnp.where(
        iota((LANES, LANES), 0) + iota((LANES, LANES), 1) == 2 * centre, 1.0, 0.0
    ).astype(BF16)
    flipped = jnp.dot(
        ff[...].reshape(3 * kernels * rows, LANES).astype(BF16), flip, preferred_element_type=F32
    )
    fr[...] = flipped.reshape(kernels, 3, rows, LANES)
    for k in range(kernels):
        fsend[0, k : k + 1, :] = fr[k, 0, 0:1, :]
        fsend[1, k : k + 1, :] = fr[k, 2, rows - 1 : rows, :]

    def filter_copy(up):
        n = 0 if up < 0 else 1
        return remote(0, 26 + n, fsend.at[n], frecv.at[n], 0, up)

    @pl.when(above)
    def _():
        filter_copy(-1).start()

    @pl.when(below)
    def _():
        filter_copy(1).start()

    blank = jnp.zeros((wide, channels), BF16)

    @pl.when(north)
    def _():
        xw[0] = blank
        gw[0] = blank
        frecv[1] = jnp.zeros(frecv.shape[1:], F32)

    @pl.when(south)
    def _():
        xw[rows + 1] = blank
        gw[rows + 1] = blank
        frecv[0] = jnp.zeros(frecv.shape[1:], F32)

    def near_block(base):
        base = jnp.broadcast_to(base, (lon_dev, 256))
        return pltpu.roll(base, 256 - 2 * lon_dev, 1, stride=1, stride_axis=0).astype(BF16)

    def far_block(filters, row, t, k):
        lane = iota((lon_dev, 128), 1)

        def part(first):
            return jnp.broadcast_to(
                filters[k, t, row : row + 1, first : first + 128], (lon_dev, 128)
            )

        low = jnp.where(lane < 2 * lon_dev, part(0), 0.0)
        high = jnp.where(lane > 2 * lon_dev, part(128), part(256))
        low = pltpu.roll(low, 0, 1, stride=1, stride_axis=0)
        high = pltpu.roll(high, 128 - lon_dev, 1, stride=1, stride_axis=0)
        return jnp.where(lane < 2 * lon_dev, low, high).astype(BF16)

    def put(dst, index, k, block):
        dst[index, pl.ds(k * lon_dev, lon_dev), :] = block

    @pl.loop(0, rows)
    def _(i):
        for t in range(3):
            for k in range(kernels):
                put(tf, i * 3 + t, k, near_block(ff[k, t, pl.ds(i, 1), 0:256]))

    forward.lifts("wait_recv")
    for up in (-1, 1):
        forward.spreads(up, "start")
    forward.pass_on(0)
    for pole in (0, 1):
        forward.fars(pole, True, "start")
    forward.pass_on(1)

    locals_[1].wait()
    inside = (iota((channels, channels), 0) // GROUP) == (iota((channels, channels), 1) // GROUP)
    for k in range(kernels):
        four = wg[k].astype(F32)
        eight = jnp.concatenate([four, four], axis=0)
        full = jnp.broadcast_to(eight[None], (channels // 8, 8, channels))
        full = full.reshape(channels, channels)
        wbd[pl.ds(k * channels, channels), :] = jnp.where(inside, full, 0.0).astype(BF16)

    @pl.loop(0, rows)
    def _(source):
        for t in range(3):
            for k in range(kernels):
                put(tb, (source + t) * 3 + t, k, near_block(fr[k, t, pl.ds(source, 1), 0:256]))

    forward.pass_on(2)
    for pole in (0, 1):

        @pl.when(north if pole == 0 else south)
        def _():
            for a in range(4):
                row = a if pole == 0 else rows - 1 - a
                for t in range(3):
                    for k in range(kernels):
                        put(te, a * 3 + t, k, far_block(ff, row, t, k))
                        put(tbe, a * 3 + t, k, far_block(fr, row, t, k))

    @pl.when(below)
    def _():
        filter_copy(-1).wait_recv()

    @pl.when(above)
    def _():
        filter_copy(1).wait_recv()

    for k in range(kernels):
        put(tb, 3 + 2, k, near_block(frecv[1, k : k + 1, 0:256]))
        put(tb, rows * 3, k, near_block(frecv[0, k : k + 1, 0:256]))

    for copy in locals_[2:]:
        copy.wait()

    def far_term(table, index, buf, row, both):
        if both:
            return jnp.dot(table[index], buf[row], preferred_element_type=F32)
        return jnp.dot(
            table[index, :, lon_dev : 3 * lon_dev],
            buf[row, lon_dev : 3 * lon_dev, :],
            preferred_element_type=F32,
        )

    def rows_in(span):
        return [first + n for first, count in span for n in range(count)]

    def scatter(ref, span, shift, at, value):
        done = 0
        for first, count in span:
            piece = value[done * lon_dev : (done + count) * lon_dev]
            ref[pl.ds(first + shift, count), at, :] = piece.reshape(count, lon_dev, channels)
            done += count

    def conv(table, offset, buf, shift, flipped, span):
        for n, i in enumerate(rows_in(span)):
            total = None
            for t in range(3):
                row = i + (2 - t if flipped else t)
                term = jnp.dot(
                    table[(i + offset) * 3 + t, :, 0:wide], buf[row], preferred_element_type=F32
                )
                total = term if total is None else total + term
            acc[n] = total

    def far_conv(table, buf, flipped, span):
        for pole in (0, 1):
            found = []
            for n, i in enumerate(rows_in(span)):
                for t in range(3):
                    source = i + (1 - t if flipped else t - 1)
                    away = source if pole == 0 else rows - 1 - source
                    a = i if pole == 0 else rows - 1 - i
                    filter_row = away if flipped else a
                    if 0 <= filter_row < 4 and away >= 0:
                        found.append((n, filter_row, t, source))
            if not found:
                continue

            @pl.when(north if pole == 0 else south)
            def _():
                for n, a, t, source in found:
                    acc[n] += far_term(table, a * 3 + t, buf, source + 1, a < 2)

    def gather(span):
        count = len(rows_in(span))
        for n in range(count):
            for k in range(kernels):
                cv[pl.ds(n * lon_dev, lon_dev), pl.ds(k * channels, channels)] = acc[
                    n, pl.ds(k * lon_dev, lon_dev), :
                ].astype(BF16)
        return pl.ds(0, count * lon_dev)

    root = 0.7978845608028654
    cubic = 0.044715

    def forward_rows(span):
        conv(tf, 0, xw, 0, False, span)
        far_conv(te, xe, False, span)
        at = gather(span)
        mixed = jnp.dot(cv[at, :], wbd[...], preferred_element_type=F32).astype(BF16)
        v = jnp.dot(mixed, wm[...], preferred_element_type=F32)
        square = v * v
        th = jnp.tanh(root * v * (1.0 + cubic * square))
        half = 0.5 * (1.0 + th)
        slope = half + 0.5 * v * (1.0 - th * th) * (root * (1.0 + 3.0 * cubic * square))
        pull = jnp.concatenate(
            [go[pl.ds(first, n)].reshape(n * lon_dev, channels) for first, n in span], axis=0
        )
        pulled = pull.astype(F32) * slope
        back = lax.dot_general(
            pulled.astype(BF16), wm[...], (((1,), (1,)), ((), ())), preferred_element_type=F32
        )
        scatter(gw, span, 1, own, back.astype(BF16))
        scatter(out_ref, span, 0, every, (v * half).astype(BF16))

    def backward_rows(span):
        conv(tb, 1, gw, 0, True, span)
        far_conv(tbe, ge, True, span)
        at = gather(span)
        total = None
        for k in range(kernels):
            lanes = pl.ds(k * channels, channels)
            term = lax.dot_general(
                cv[at, lanes], wbd[lanes, :], (((1,), (1,)), ((), ())), preferred_element_type=F32
            )
            total = term if total is None else total + term
        scatter(gin_ref, span, 0, every, total.astype(BF16))

    def finish(phase):
        for g in range(3):
            phase.sent(g)
        phase.lifts("wait_send")
        for up in (-1, 1):
            phase.spreads(up, "wait_send")
        for pole in (0, 1):
            for early in (True, False):
                phase.fars(pole, early, "wait_send")

    outer, middle = ((0, 2), (6, 2)), ((2, 4),)
    forward.arrive(0)
    forward.arrive(1)
    for up in (1, -1):
        forward.spreads(up, "wait_recv")
    for pole in (0, 1):
        forward.fars(pole, True, "wait_recv")
    forward_rows(outer)

    @pl.when(above)
    def _():
        run(backward.lift(-1), "start")

    @pl.when(below)
    def _():
        run(backward.lift(1), "start")

    run(backward.group(0), "start")
    run(backward.group(1), "start")
    forward.arrive(2)
    for pole in (0, 1):
        forward.fars(pole, False, "wait_recv")
    forward_rows(middle)
    for pole in (0, 1):
        backward.fars(pole, False, "start")
    run(backward.group(2), "start")
    backward.lifts("wait_recv")
    for up in (-1, 1):
        backward.spreads(up, "start")
    backward.pass_on(0)
    for pole in (0, 1):
        backward.fars(pole, True, "start")
    backward.pass_on(1)
    finish(forward)

    @pl.when(above)
    def _():
        filter_copy(-1).wait_send()

    @pl.when(below)
    def _():
        filter_copy(1).wait_send()

    backward.pass_on(2)
    for g in range(3):
        backward.arrive(g)
    for early in (True, False):
        for pole in (0, 1):
            backward.fars(pole, early, "wait_recv")
    backward_rows(middle)
    for up in (1, -1):
        backward.spreads(up, "wait_recv")
    backward_rows(outer)
    finish(backward)


def body(n_lon, n_lat, inputs, psi_raw, widths, w_group, w_mix, grad_out):
    rows, lon_dev, channels = inputs.shape
    kernels = psi_raw.shape[0]
    wide = 5 * lon_dev
    depth = kernels * lon_dev
    copies = 30
    psi_raw = jnp.transpose(psi_raw, (0, 2, 1, 3))
    anywhere = pl.BlockSpec(memory_space=pltpu.HBM)
    vmem = pl.BlockSpec(memory_space=pltpu.VMEM)
    shape = jax.ShapeDtypeStruct(inputs.shape, BF16)
    both = pl.pallas_call(
        functools.partial(kernel, n_lon, n_lat),
        name="disco",
        out_shape=pltpu.VMEM((2,) + inputs.shape, BF16),
        in_specs=[
            anywhere, anywhere, pl.BlockSpec(memory_space=pltpu.SMEM),
            anywhere, anywhere, anywhere,
        ],
        out_specs=vmem,
        scratch_shapes=[
            pltpu.VMEM(psi_raw.shape, F32),
            pltpu.VMEM(w_group.shape, BF16),
            pltpu.VMEM(w_mix.shape, BF16),
            pltpu.VMEM(grad_out.shape, BF16),
            pltpu.VMEM((rows + 2, wide, channels), BF16),
            pltpu.VMEM((rows + 2, wide, channels), BF16),
            pltpu.VMEM((rows + 2, 4 * lon_dev, channels), BF16),
            pltpu.VMEM((rows + 2, 4 * lon_dev, channels), BF16),
            pltpu.VMEM((kernels, 3, rows, LANES), F32),
            pltpu.VMEM((kernels, 3, rows, LANES), F32),
            pltpu.VMEM((2, 8, LANES), F32),
            pltpu.VMEM((2, 8, LANES), F32),
            pltpu.VMEM((rows * 3, depth, 256), BF16),
            pltpu.VMEM(((rows + 2) * 3, depth, 256), BF16),
            pltpu.VMEM((12, depth, 4 * lon_dev), BF16),
            pltpu.VMEM((12, depth, 4 * lon_dev), BF16),
            pltpu.VMEM((kernels * channels, channels), BF16),
            pltpu.VMEM((4 * lon_dev, kernels * channels), BF16),
            pltpu.VMEM((4, depth, channels), F32),
            pltpu.SemaphoreType.DMA((5,)),
            pltpu.SemaphoreType.DMA((2, copies)),
            pltpu.SemaphoreType.DMA((2, copies)),
        ],
        compiler_params=pltpu.CompilerParams(
            collective_id=0, has_side_effects=True
        ),
        cost_estimate=pl.CostEstimate(
            flops=4_000_000_000, bytes_accessed=2_000_000, transcendentals=65536
        ),
    )(inputs, psi_raw, widths, w_group, w_mix, grad_out)
    return both[0], both[1]


def solution(mesh):
    return jax.shard_map(
        functools.partial(body, mesh.shape["lon"], mesh.shape["lat"]),
        mesh=mesh,
        in_specs=(
            P("lat", "lon", None),
            P(None, "lat", None, None),
            P("lat"),
            P(),
            P(),
            P("lat", "lon", None),
        ),
        out_specs=(P("lat", "lon", None), P("lat", "lon", None)),
        check_vma=False,
    )
```

```python
import functools

import jax
import jax.numpy as jnp
from jax import lax
from jax.experimental import pallas as pl
from jax.experimental.pallas import tpu as pltpu
from jax.sharding import PartitionSpec as P

GROUP = 4
SMAX = 4
LANES = 384
NEAR = (-1, 1, -2, 2)
SLOT = {-2: 0, -1: 1, 0: 2, 1: 3, 2: 4}
FAR_SLOT = {-4: 0, -3: 1, 3: 2, 4: 3}
MESH = pl.DeviceIdType.MESH
F32 = jnp.float32
BF16 = jnp.bfloat16


def iota(shape, axis):
    return lax.broadcasted_iota(jnp.int32, shape, axis)


def kernel(
    n_lon, n_lat,
    x_hbm, psi_hbm, widths, wg_hbm, wm_hbm, go_hbm,
    both_ref,
    psi, wg, wm, go, xw, gw, xe, ge, ff, fr, fsend, frecv, tf, tb, te, tbe, wbd, cv, acc,
    local_sem, send_sem, recv_sem,
):
    out_ref, gin_ref = both_ref.at[0], both_ref.at[1]
    rows, lon_dev, channels = x_hbm.shape
    kernels, taps = psi_hbm.shape[0], psi_hbm.shape[3]
    centre = SMAX * lon_dev
    wide = lon_dev * 5
    lon, lat = lax.axis_index("lon"), lax.axis_index("lat")
    north, south = lat == 0, lat == n_lat - 1
    above, below = jnp.logical_not(north), jnp.logical_not(south)

    def at_lon(by):
        return lax.rem(lon + (by + n_lon), n_lon)

    barrier = pltpu.get_barrier_semaphore()

    def greet(by, up):
        pl.semaphore_signal(
            barrier, inc=1, device_id={"lon": at_lon(by), "lat": lat + up}, device_id_type=MESH
        )

    for by in NEAR:
        greet(by, 0)

    @pl.when(above)
    def _():
        greet(0, -1)

    @pl.when(below)
    def _():
        greet(0, 1)

    polar = jnp.logical_or(north, south)

    @pl.when(polar)
    def _():
        for by in (-3, 3):
            greet(by, 0)

    own = pl.ds(SLOT[0] * lon_dev, lon_dev)
    every = pl.ds(0, lon_dev)
    locals_ = [
        pltpu.make_async_copy(psi_hbm, psi, local_sem.at[0]),
        pltpu.make_async_copy(wg_hbm, wg, local_sem.at[1]),
        pltpu.make_async_copy(wm_hbm, wm, local_sem.at[2]),
        pltpu.make_async_copy(go_hbm, go, local_sem.at[3]),
        pltpu.make_async_copy(x_hbm, xw.at[pl.ds(1, rows), own, :], local_sem.at[4]),
    ]
    for copy in locals_:
        copy.start()

    side = 1 - 2 * lax.rem(lon, 2)

    def slot_at(by):
        return pl.ds(pl.multiple_of((by + 2) * lon_dev, lon_dev), lon_dev)

    def remote(phase, index, src, dst, by, up=0):
        return pltpu.make_async_remote_copy(
            src_ref=src,
            dst_ref=dst,
            send_sem=send_sem.at[phase, index],
            recv_sem=recv_sem.at[phase, index],
            device_id={"lon": at_lon(by), "lat": lat + up},
            device_id_type=MESH,
        )

    def slot(by):
        return pl.ds(SLOT[by] * lon_dev, lon_dev)

    def far_slot(by):
        return pl.ds(FAR_SLOT[by] * lon_dev, lon_dev)

    class Phase:
        def __init__(self, phase, source, first, at, buf, far_buf, groups, far_count, routes):
            self.phase, self.source, self.first, self.at = phase, source, first, at
            self.buf, self.far_buf, self.groups = buf, far_buf, groups
            self.far_count, self.routes = far_count, routes

        def first_of(self, g):
            row, count = self.groups[g]
            return jnp.where(south, rows - row - count, row)

        def rows_of(self, row, count):
            return self.source.at[pl.ds(self.first + row, count), self.at, :]

        def part(self, g, n, by, at):
            row, count = self.first_of(g), self.groups[g][1]
            return remote(
                self.phase, g * 4 + n, self.rows_of(row, count),
                self.buf.at[pl.ds(1 + row, count), at, :], by,
            )

        def group(self, g):
            found = [
                self.part(g, 0, side, slot_at(-side)),
                self.part(g, 2, -2 * side, slot_at(2 * side)),
                self.part(g, 3, 2 * side, slot_at(-2 * side)),
            ]
            if self.routes[g] is None:
                found.append(self.part(g, 1, -side, slot_at(side)))
            return found

        def relay(self, g):
            rows_ = pl.ds(1 + self.first_of(g), self.groups[g][1])
            if self.routes[g] == "plane":
                source, target, by = side, -side, 2 * side
            else:
                source, target, by = 2 * side, side, side
            return [
                remote(
                    self.phase, g * 4 + 1, self.buf.at[rows_, slot_at(source), :],
                    self.buf.at[rows_, slot_at(target), :], by,
                )
            ]

        def landed(self, g, which):
            ats = {0: side, 1: -side, 2: 2 * side, 3: -2 * side}
            return [self.part(g, n, side, slot_at(ats[n])) for n in which]

        def pass_on(self, g):
            run(self.landed(g, (0, 2, 3)), "wait_recv")
            if self.routes[g]:
                run(self.relay(g), "start")

        def arrive(self, g):
            run(self.landed(g, (1,)), "wait_recv")

        def sent(self, g):
            run(self.group(g), "wait_send")
            if self.routes[g]:
                run(self.relay(g), "wait_send")

        def lift(self, up):
            row, target = (0, rows + 1) if up < 0 else (rows - 1, 0)
            return [
                remote(
                    self.phase, 12 + (0 if up < 0 else 1), self.rows_of(row, 1),
                    self.buf.at[pl.ds(target, 1), own, :], 0, up,
                )
            ]

        def spread(self, up):
            target = rows + 1 if up < 0 else 0
            return [
                remote(
                    self.phase, 14 + n + (0 if up < 0 else 4),
                    self.buf.at[pl.ds(target, 1), own, :],
                    self.buf.at[pl.ds(target, 1), slot(-by), :], by,
                )
                for n, by in enumerate(NEAR)
            ]

        def far(self, pole, early):
            count = self.far_count
            if early:
                rows_ = pl.ds(1 if pole == 0 else 1 + rows - count, count)
                return [
                    remote(
                        self.phase, 22 + 2 * (reach - 3) + (s + 1) // 2,
                        self.buf.at[rows_, slot(2 * s), :],
                        self.far_buf.at[rows_, far_slot(s * reach), :], -s * (reach - 2),
                    )
                    for reach in (3, 4)
                    for s in (-1, 1)
                ]
            row = count if pole == 0 else rows - count - 2
            return [
                remote(
                    self.phase, 28 + (s + 1) // 2, self.rows_of(row, 2),
                    self.far_buf.at[pl.ds(1 + row, 2), far_slot(-3 * s), :], 3 * s,
                )
                for s in (-1, 1)
            ]

        def lifts(self, what):
            for up in (-1, 1):
                ok = (above if up < 0 else below) if what != "wait_recv" else (
                    below if up < 0 else above
                )

                @pl.when(ok)
                def _():
                    run(self.lift(up), what)

        def spreads(self, up, what):
            @pl.when(below if up < 0 else above)
            def _():
                run(self.spread(up), what)

        def fars(self, pole, early, what):
            @pl.when(north if pole == 0 else south)
            def _():
                run(self.far(pole, early), what)

    def run(copies, what):
        for copy in copies:
            getattr(copy, what)()

    forward = Phase(0, x_hbm, 0, every, xw, xe, ((0, 3), (5, 3), (3, 2)), 3, ('pair', 'plane', 'pair'))
    backward = Phase(1, gw, 1, own, gw, ge, ((0, 2), (6, 2), (2, 4)), 2, ('plane', 'plane', None))

    pl.semaphore_wait(
        barrier,
        4 + above.astype(jnp.int32) + below.astype(jnp.int32) + 2 * polar.astype(jnp.int32),
    )
    forward.lifts("start")
    run(forward.group(0), "start")
    run(forward.group(1), "start")
    for pole in (0, 1):
        forward.fars(pole, False, "start")
    run(forward.group(2), "start")

    locals_[0].wait()
    line = iota((rows, LANES), 0)
    reach = jnp.zeros((rows, LANES), jnp.int32)
    for i in range(rows):
        reach = jnp.where(line == i, widths[i] * lon_dev, reach)
    keep = jnp.where(
        jnp.abs(iota((rows, LANES), 1) - centre) <= reach,
        lax.rsqrt(3.0 * (2.0 * reach.astype(F32) + 1.0)),
        0.0,
    )
    ff[:, :, :, 256:LANES] = jnp.zeros((kernels, 3, rows, LANES - 256), F32)
    for k in range(kernels):
        for t in range(3):
            ff[k, t, :, 0:taps] = psi[k, t] * keep[:, 0:taps]


    flip = jnp.where(
        iota((LANES, LANES), 0) + iota((LANES, LANES), 1) == 2 * centre, 1.0, 0.0
    ).astype(BF16)
    flipped = jnp.dot(
        ff[...].reshape(3 * kernels * rows, LANES).astype(BF16), flip, preferred_element_type=F32
    )
    fr[...] = flipped.reshape(kernels, 3, rows, LANES)
    for k in range(kernels):
        fsend[0, k : k + 1, :] = fr[k, 0, 0:1, :]
        fsend[1, k : k + 1, :] = fr[k, 2, rows - 1 : rows, :]

    def filter_copy(up):
        n = 0 if up < 0 else 1
        return remote(0, 26 + n, fsend.at[n], frecv.at[n], 0, up)

    @pl.when(above)
    def _():
        filter_copy(-1).start()

    @pl.when(below)
    def _():
        filter_copy(1).start()

    blank = jnp.zeros((wide, channels), BF16)

    @pl.when(north)
    def _():
        xw[0] = blank
        gw[0] = blank
        frecv[1] = jnp.zeros(frecv.shape[1:], F32)

    @pl.when(south)
    def _():
        xw[rows + 1] = blank
        gw[rows + 1] = blank
        frecv[0] = jnp.zeros(frecv.shape[1:], F32)

    def near_block(base):
        base = jnp.broadcast_to(base, (lon_dev, 256))
        return pltpu.roll(base, 256 - 2 * lon_dev, 1, stride=1, stride_axis=0).astype(BF16)

    def far_block(filters, row, t, k):
        lane = iota((lon_dev, 128), 1)

        def part(first):
            return jnp.broadcast_to(
                filters[k, t, row : row + 1, first : first + 128], (lon_dev, 128)
            )

        low = jnp.where(lane < 2 * lon_dev, part(0), 0.0)
        high = jnp.where(lane > 2 * lon_dev, part(128), part(256))
        low = pltpu.roll(low, 0, 1, stride=1, stride_axis=0)
        high = pltpu.roll(high, 128 - lon_dev, 1, stride=1, stride_axis=0)
        return jnp.where(lane < 2 * lon_dev, low, high).astype(BF16)

    def put(dst, index, k, block):
        dst[index, pl.ds(k * lon_dev, lon_dev), :] = block

    @pl.loop(0, rows)
    def _(i):
        for t in range(3):
            for k in range(kernels):
                put(tf, i * 3 + t, k, near_block(ff[k, t, pl.ds(i, 1), 0:256]))

    forward.lifts("wait_recv")
    for up in (-1, 1):
        forward.spreads(up, "start")
    forward.pass_on(0)
    for pole in (0, 1):
        forward.fars(pole, True, "start")
    forward.pass_on(1)

    locals_[1].wait()
    inside = (iota((channels, channels), 0) // GROUP) == (iota((channels, channels), 1) // GROUP)
    for k in range(kernels):
        four = wg[k].astype(F32)
        eight = jnp.concatenate([four, four], axis=0)
        full = jnp.broadcast_to(eight[None], (channels // 8, 8, channels))
        full = full.reshape(channels, channels)
        wbd[pl.ds(k * channels, channels), :] = jnp.where(inside, full, 0.0).astype(BF16)

    @pl.loop(0, rows)
    def _(source):
        for t in range(3):
            for k in range(kernels):
                put(tb, (source + t) * 3 + t, k, near_block(fr[k, t, pl.ds(source, 1), 0:256]))

    forward.pass_on(2)
    for pole in (0, 1):

        @pl.when(north if pole == 0 else south)
        def _():
            for a in range(4):
                row = a if pole == 0 else rows - 1 - a
                for t in range(3):
                    for k in range(kernels):
                        put(te, a * 3 + t, k, far_block(ff, row, t, k))
                        put(tbe, a * 3 + t, k, far_block(fr, row, t, k))

    @pl.when(below)
    def _():
        filter_copy(-1).wait_recv()

    @pl.when(above)
    def _():
        filter_copy(1).wait_recv()

    for k in range(kernels):
        put(tb, 3 + 2, k, near_block(frecv[1, k : k + 1, 0:256]))
        put(tb, rows * 3, k, near_block(frecv[0, k : k + 1, 0:256]))

    for copy in locals_[2:]:
        copy.wait()

    def far_term(table, index, buf, row, both):
        if both:
            return jnp.dot(table[index], buf[row], preferred_element_type=F32)
        return jnp.dot(
            table[index, :, lon_dev : 3 * lon_dev],
            buf[row, lon_dev : 3 * lon_dev, :],
            preferred_element_type=F32,
        )

    def rows_in(span):
        return [first + n for first, count in span for n in range(count)]

    def scatter(ref, span, shift, at, value):
        done = 0
        for first, count in span:
            piece = value[done * lon_dev : (done + count) * lon_dev]
            ref[pl.ds(first + shift, count), at, :] = piece.reshape(count, lon_dev, channels)
            done += count

    def conv(table, offset, buf, shift, flipped, span):
        for n, i in enumerate(rows_in(span)):
            total = None
            for t in range(3):
                row = i + (2 - t if flipped else t)
                term = jnp.dot(
                    table[(i + offset) * 3 + t, :, 0:wide], buf[row], preferred_element_type=F32
                )
                total = term if total is None else total + term
            acc[n] = total

    def far_conv(table, buf, flipped, span):
        for pole in (0, 1):
            found = []
            for n, i in enumerate(rows_in(span)):
                for t in range(3):
                    source = i + (1 - t if flipped else t - 1)
                    away = source if pole == 0 else rows - 1 - source
                    a = i if pole == 0 else rows - 1 - i
                    filter_row = away if flipped else a
                    if 0 <= filter_row < 4 and away >= 0:
                        found.append((n, filter_row, t, source))
            if not found:
                continue

            @pl.when(north if pole == 0 else south)
            def _():
                for n, a, t, source in found:
                    acc[n] += far_term(table, a * 3 + t, buf, source + 1, a < 2)

    def gather(span):
        count = len(rows_in(span))
        for n in range(count):
            for k in range(kernels):
                cv[pl.ds(n * lon_dev, lon_dev), pl.ds(k * channels, channels)] = acc[
                    n, pl.ds(k * lon_dev, lon_dev), :
                ].astype(BF16)
        return pl.ds(0, count * lon_dev)

    root = 0.7978845608028654
    cubic = 0.044715

    def forward_rows(span):
        conv(tf, 0, xw, 0, False, span)
        far_conv(te, xe, False, span)
        at = gather(span)
        mixed = jnp.dot(cv[at, :], wbd[...], preferred_element_type=F32).astype(BF16)
        v = jnp.dot(mixed, wm[...], preferred_element_type=F32)
        square = v * v
        th = jnp.tanh(root * v * (1.0 + cubic * square))
        half = 0.5 * (1.0 + th)
        slope = half + 0.5 * v * (1.0 - th * th) * (root * (1.0 + 3.0 * cubic * square))
        pull = jnp.concatenate(
            [go[pl.ds(first, n)].reshape(n * lon_dev, channels) for first, n in span], axis=0
        )
        pulled = pull.astype(F32) * slope
        back = lax.dot_general(
            pulled.astype(BF16), wm[...], (((1,), (1,)), ((), ())), preferred_element_type=F32
        )
        scatter(gw, span, 1, own, back.astype(BF16))
        scatter(out_ref, span, 0, every, (v * half).astype(BF16))

    def backward_rows(span):
        conv(tb, 1, gw, 0, True, span)
        far_conv(tbe, ge, True, span)
        at = gather(span)
        total = None
        for k in range(kernels):
            lanes = pl.ds(k * channels, channels)
            term = lax.dot_general(
                cv[at, lanes], wbd[lanes, :], (((1,), (1,)), ((), ())), preferred_element_type=F32
            )
            total = term if total is None else total + term
        scatter(gin_ref, span, 0, every, total.astype(BF16))

    def finish(phase):
        for g in range(3):
            phase.sent(g)
        phase.lifts("wait_send")
        for up in (-1, 1):
            phase.spreads(up, "wait_send")
        for pole in (0, 1):
            for early in (True, False):
                phase.fars(pole, early, "wait_send")

    outer, middle = ((0, 2), (6, 2)), ((2, 4),)
    forward.arrive(0)
    forward.arrive(1)
    for up in (1, -1):
        forward.spreads(up, "wait_recv")
    for pole in (0, 1):
        forward.fars(pole, True, "wait_recv")
    forward_rows(outer)

    @pl.when(above)
    def _():
        run(backward.lift(-1), "start")

    @pl.when(below)
    def _():
        run(backward.lift(1), "start")

    run(backward.group(0), "start")
    run(backward.group(1), "start")
    forward.arrive(2)
    for pole in (0, 1):
        forward.fars(pole, False, "wait_recv")
    forward_rows(middle)
    for pole in (0, 1):
        backward.fars(pole, False, "start")
    run(backward.group(2), "start")
    backward.lifts("wait_recv")
    for up in (-1, 1):
        backward.spreads(up, "start")
    backward.pass_on(0)
    for pole in (0, 1):
        backward.fars(pole, True, "start")
    backward.pass_on(1)
    finish(forward)

    @pl.when(above)
    def _():
        filter_copy(-1).wait_send()

    @pl.when(below)
    def _():
        filter_copy(1).wait_send()

    backward.pass_on(2)
    for g in range(3):
        backward.arrive(g)
    for early in (True, False):
        for pole in (0, 1):
            backward.fars(pole, early, "wait_recv")
    backward_rows(middle)
    for up in (1, -1):
        backward.spreads(up, "wait_recv")
    backward_rows(outer)
    finish(backward)


def body(n_lon, n_lat, inputs, psi_raw, widths, w_group, w_mix, grad_out):
    rows, lon_dev, channels = inputs.shape
    kernels = psi_raw.shape[0]
    wide = 5 * lon_dev
    depth = kernels * lon_dev
    copies = 30
    psi_raw = jnp.transpose(psi_raw, (0, 2, 1, 3))
    anywhere = pl.BlockSpec(memory_space=pltpu.HBM)
    vmem = pl.BlockSpec(memory_space=pltpu.VMEM)
    shape = jax.ShapeDtypeStruct(inputs.shape, BF16)
    both = pl.pallas_call(
        functools.partial(kernel, n_lon, n_lat),
        name="disco",
        out_shape=pltpu.VMEM((2,) + inputs.shape, BF16),
        in_specs=[
            anywhere, anywhere, pl.BlockSpec(memory_space=pltpu.SMEM),
            anywhere, anywhere, anywhere,
        ],
        out_specs=vmem,
        scratch_shapes=[
            pltpu.VMEM(psi_raw.shape, F32),
            pltpu.VMEM(w_group.shape, BF16),
            pltpu.VMEM(w_mix.shape, BF16),
            pltpu.VMEM(grad_out.shape, BF16),
            pltpu.VMEM((rows + 2, wide, channels), BF16),
            pltpu.VMEM((rows + 2, wide, channels), BF16),
            pltpu.VMEM((rows + 2, 4 * lon_dev, channels), BF16),
            pltpu.VMEM((rows + 2, 4 * lon_dev, channels), BF16),
            pltpu.VMEM((kernels, 3, rows, LANES), F32),
            pltpu.VMEM((kernels, 3, rows, LANES), F32),
            pltpu.VMEM((2, 8, LANES), F32),
            pltpu.VMEM((2, 8, LANES), F32),
            pltpu.VMEM((rows * 3, depth, 256), BF16),
            pltpu.VMEM(((rows + 2) * 3, depth, 256), BF16),
            pltpu.VMEM((12, depth, 4 * lon_dev), BF16),
            pltpu.VMEM((12, depth, 4 * lon_dev), BF16),
            pltpu.VMEM((kernels * channels, channels), BF16),
            pltpu.VMEM((4 * lon_dev, kernels * channels), BF16),
            pltpu.VMEM((4, depth, channels), F32),
            pltpu.SemaphoreType.DMA((5,)),
            pltpu.SemaphoreType.DMA((2, copies)),
            pltpu.SemaphoreType.DMA((2, copies)),
        ],
        compiler_params=pltpu.CompilerParams(
            collective_id=0, has_side_effects=True
        ),
        cost_estimate=pl.CostEstimate(
            flops=4_000_000_000, bytes_accessed=2_000_000, transcendentals=65536
        ),
    )(inputs, psi_raw, widths, w_group, w_mix, grad_out)
    return both[0], both[1]


def solution(mesh):
    return jax.shard_map(
        functools.partial(body, mesh.shape["lon"], mesh.shape["lat"]),
        mesh=mesh,
        in_specs=(
            P("lat", "lon", None),
            P(None, "lat", None, None),
            P("lat"),
            P(),
            P(),
            P("lat", "lon", None),
        ),
        out_specs=(P("lat", "lon", None), P("lat", "lon", None)),
        check_vma=False,
    )
```

```python
import functools

import jax
import jax.numpy as jnp
from jax import lax
from jax.experimental import pallas as pl
from jax.experimental.pallas import tpu as pltpu
from jax.sharding import PartitionSpec as P

GROUP = 4
SMAX = 4
LANES = 384
NEAR = (-1, 1, -2, 2)
SLOT = {-2: 0, -1: 1, 0: 2, 1: 3, 2: 4}
FAR_SLOT = {-4: 0, -3: 1, 3: 2, 4: 3}
MESH = pl.DeviceIdType.MESH
F32 = jnp.float32
BF16 = jnp.bfloat16


def iota(shape, axis):
    return lax.broadcasted_iota(jnp.int32, shape, axis)


def kernel(
    n_lon, n_lat,
    x_hbm, psi_hbm, widths, wg_hbm, wm_hbm, go_hbm,
    both_ref,
    psi, wg, wm, go, xw, gw, xe, ge, ff, fr, fsend, frecv, tf, tb, te, tbe, wbd, cv, acc,
    local_sem, send_sem, recv_sem,
):
    out_ref, gin_ref = both_ref.at[0], both_ref.at[1]
    rows, lon_dev, channels = x_hbm.shape
    kernels, taps = psi_hbm.shape[0], psi_hbm.shape[3]
    centre = SMAX * lon_dev
    wide = lon_dev * 5
    lon, lat = lax.axis_index("lon"), lax.axis_index("lat")
    north, south = lat == 0, lat == n_lat - 1
    above, below = jnp.logical_not(north), jnp.logical_not(south)

    def at_lon(by):
        return lax.rem(lon + (by + n_lon), n_lon)

    barrier = pltpu.get_barrier_semaphore()

    def greet(by, up):
        pl.semaphore_signal(
            barrier, inc=1, device_id={"lon": at_lon(by), "lat": lat + up}, device_id_type=MESH
        )

    for by in NEAR:
        greet(by, 0)

    @pl.when(above)
    def _():
        greet(0, -1)

    @pl.when(below)
    def _():
        greet(0, 1)

    polar = jnp.logical_or(north, south)

    @pl.when(polar)
    def _():
        for by in (-3, 3):
            greet(by, 0)

    own = pl.ds(SLOT[0] * lon_dev, lon_dev)
    every = pl.ds(0, lon_dev)
    locals_ = [
        pltpu.make_async_copy(psi_hbm, psi, local_sem.at[0]),
        pltpu.make_async_copy(wg_hbm, wg, local_sem.at[1]),
        pltpu.make_async_copy(wm_hbm, wm, local_sem.at[2]),
        pltpu.make_async_copy(go_hbm, go, local_sem.at[3]),
        pltpu.make_async_copy(x_hbm, xw.at[pl.ds(1, rows), own, :], local_sem.at[4]),
    ]
    for copy in locals_:
        copy.start()

    side = 1 - 2 * lax.rem(lon, 2)

    def slot_at(by):
        return pl.ds(pl.multiple_of((by + 2) * lon_dev, lon_dev), lon_dev)

    def remote(phase, index, src, dst, by, up=0):
        return pltpu.make_async_remote_copy(
            src_ref=src,
            dst_ref=dst,
            send_sem=send_sem.at[phase, index],
            recv_sem=recv_sem.at[phase, index],
            device_id={"lon": at_lon(by), "lat": lat + up},
            device_id_type=MESH,
        )

    def slot(by):
        return pl.ds(SLOT[by] * lon_dev, lon_dev)

    def far_slot(by):
        return pl.ds(FAR_SLOT[by] * lon_dev, lon_dev)

    class Phase:
        def __init__(self, phase, source, first, at, buf, far_buf, groups, far_count, routes):
            self.phase, self.source, self.first, self.at = phase, source, first, at
            self.buf, self.far_buf, self.groups = buf, far_buf, groups
            self.far_count, self.routes = far_count, routes

        def first_of(self, g):
            row, count = self.groups[g]
            return jnp.where(south, rows - row - count, row)

        def rows_of(self, row, count):
            return self.source.at[pl.ds(self.first + row, count), self.at, :]

        def part(self, g, n, by, at):
            row, count = self.first_of(g), self.groups[g][1]
            return remote(
                self.phase, g * 4 + n, self.rows_of(row, count),
                self.buf.at[pl.ds(1 + row, count), at, :], by,
            )

        def group(self, g):
            found = [
                self.part(g, 0, side, slot_at(-side)),
                self.part(g, 2, -2 * side, slot_at(2 * side)),
                self.part(g, 3, 2 * side, slot_at(-2 * side)),
            ]
            if self.routes[g] is None:
                found.insert(0, self.part(g, 1, -side, slot_at(side)))
            return found

        def relay(self, g):
            rows_ = pl.ds(1 + self.first_of(g), self.groups[g][1])
            if self.routes[g] == "plane":
                source, target, by = side, -side, 2 * side
            else:
                source, target, by = 2 * side, side, side
            return [
                remote(
                    self.phase, g * 4 + 1, self.buf.at[rows_, slot_at(source), :],
                    self.buf.at[rows_, slot_at(target), :], by,
                )
            ]

        def landed(self, g, which):
            ats = {0: side, 1: -side, 2: 2 * side, 3: -2 * side}
            return [self.part(g, n, side, slot_at(ats[n])) for n in which]

        def pass_on(self, g):
            run(self.landed(g, (0, 2, 3)), "wait_recv")
            if self.routes[g]:
                run(self.relay(g), "start")

        def arrive(self, g):
            run(self.landed(g, (1,)), "wait_recv")

        def sent(self, g):
            run(self.group(g), "wait_send")
            if self.routes[g]:
                run(self.relay(g), "wait_send")

        def lift(self, up):
            row, target = (0, rows + 1) if up < 0 else (rows - 1, 0)
            return [
                remote(
                    self.phase, 12 + (0 if up < 0 else 1), self.rows_of(row, 1),
                    self.buf.at[pl.ds(target, 1), own, :], 0, up,
                )
            ]

        def spread(self, up):
            target = rows + 1 if up < 0 else 0
            return [
                remote(
                    self.phase, 14 + n + (0 if up < 0 else 4),
                    self.buf.at[pl.ds(target, 1), own, :],
                    self.buf.at[pl.ds(target, 1), slot(-by), :], by,
                )
                for n, by in enumerate(NEAR)
            ]

        def far(self, pole, early):
            count = self.far_count
            if early:
                rows_ = pl.ds(1 if pole == 0 else 1 + rows - count, count)
                return [
                    remote(
                        self.phase, 22 + 2 * (reach - 3) + (s + 1) // 2,
                        self.buf.at[rows_, slot(2 * s), :],
                        self.far_buf.at[rows_, far_slot(s * reach), :], -s * (reach - 2),
                    )
                    for reach in (3, 4)
                    for s in (-1, 1)
                ]
            row = count if pole == 0 else rows - count - 2
            return [
                remote(
                    self.phase, 28 + (s + 1) // 2, self.rows_of(row, 2),
                    self.far_buf.at[pl.ds(1 + row, 2), far_slot(-3 * s), :], 3 * s,
                )
                for s in (-1, 1)
            ]

        def lifts(self, what):
            for up in (-1, 1):
                ok = (above if up < 0 else below) if what != "wait_recv" else (
                    below if up < 0 else above
                )

                @pl.when(ok)
                def _():
                    run(self.lift(up), what)

        def spreads(self, up, what):
            @pl.when(below if up < 0 else above)
            def _():
                run(self.spread(up), what)

        def fars(self, pole, early, what):
            @pl.when(north if pole == 0 else south)
            def _():
                run(self.far(pole, early), what)

    def run(copies, what):
        for copy in copies:
            getattr(copy, what)()

    forward = Phase(0, x_hbm, 0, every, xw, xe, ((0, 3), (5, 3), (3, 2)), 3, ('pair', 'plane', 'pair'))
    backward = Phase(1, gw, 1, own, gw, ge, ((0, 2), (6, 2), (2, 4)), 2, ('plane', 'plane', None))

    pl.semaphore_wait(
        barrier,
        4 + above.astype(jnp.int32) + below.astype(jnp.int32) + 2 * polar.astype(jnp.int32),
    )
    forward.lifts("start")
    run(forward.group(0), "start")
    run(forward.group(1), "start")
    run(forward.group(2), "start")
    for pole in (0, 1):
        forward.fars(pole, False, "start")

    locals_[0].wait()
    line = iota((rows, LANES), 0)
    reach = jnp.zeros((rows, LANES), jnp.int32)
    for i in range(rows):
        reach = jnp.where(line == i, widths[i] * lon_dev, reach)
    keep = jnp.where(
        jnp.abs(iota((rows, LANES), 1) - centre) <= reach,
        lax.rsqrt(3.0 * (2.0 * reach.astype(F32) + 1.0)),
        0.0,
    )
    ff[:, :, :, 256:LANES] = jnp.zeros((kernels, 3, rows, LANES - 256), F32)
    for k in range(kernels):
        for t in range(3):
            ff[k, t, :, 0:taps] = psi[k, t] * keep[:, 0:taps]


    flip = jnp.where(
        iota((LANES, LANES), 0) + iota((LANES, LANES), 1) == 2 * centre, 1.0, 0.0
    ).astype(BF16)
    flipped = jnp.dot(
        ff[...].reshape(3 * kernels * rows, LANES).astype(BF16), flip, preferred_element_type=F32
    )
    fr[...] = flipped.reshape(kernels, 3, rows, LANES)
    for k in range(kernels):
        fsend[0, k : k + 1, :] = fr[k, 0, 0:1, :]
        fsend[1, k : k + 1, :] = fr[k, 2, rows - 1 : rows, :]

    def filter_copy(up):
        n = 0 if up < 0 else 1
        return remote(0, 26 + n, fsend.at[n], frecv.at[n], 0, up)

    @pl.when(above)
    def _():
        filter_copy(-1).start()

    @pl.when(below)
    def _():
        filter_copy(1).start()

    blank = jnp.zeros((wide, channels), BF16)

    @pl.when(north)
    def _():
        xw[0] = blank
        gw[0] = blank
        frecv[1] = jnp.zeros(frecv.shape[1:], F32)

    @pl.when(south)
    def _():
        xw[rows + 1] = blank
        gw[rows + 1] = blank
        frecv[0] = jnp.zeros(frecv.shape[1:], F32)

    def near_block(base):
        base = jnp.broadcast_to(base, (lon_dev, 256))
        return pltpu.roll(base, 256 - 2 * lon_dev, 1, stride=1, stride_axis=0).astype(BF16)

    def far_block(filters, row, t, k):
        lane = iota((lon_dev, 128), 1)

        def part(first):
            return jnp.broadcast_to(
                filters[k, t, row : row + 1, first : first + 128], (lon_dev, 128)
            )

        low = jnp.where(lane < 2 * lon_dev, part(0), 0.0)
        high = jnp.where(lane > 2 * lon_dev, part(128), part(256))
        low = pltpu.roll(low, 0, 1, stride=1, stride_axis=0)
        high = pltpu.roll(high, 128 - lon_dev, 1, stride=1, stride_axis=0)
        return jnp.where(lane < 2 * lon_dev, low, high).astype(BF16)

    def put(dst, index, k, block):
        dst[index, pl.ds(k * lon_dev, lon_dev), :] = block

    @pl.loop(0, rows)
    def _(i):
        for t in range(3):
            for k in range(kernels):
                put(tf, i * 3 + t, k, near_block(ff[k, t, pl.ds(i, 1), 0:256]))

    forward.lifts("wait_recv")
    for up in (-1, 1):
        forward.spreads(up, "start")
    forward.pass_on(0)
    for pole in (0, 1):
        forward.fars(pole, True, "start")
    forward.pass_on(1)

    locals_[1].wait()
    inside = (iota((channels, channels), 0) // GROUP) == (iota((channels, channels), 1) // GROUP)
    for k in range(kernels):
        four = wg[k].astype(F32)
        eight = jnp.concatenate([four, four], axis=0)
        full = jnp.broadcast_to(eight[None], (channels // 8, 8, channels))
        full = full.reshape(channels, channels)
        wbd[pl.ds(k * channels, channels), :] = jnp.where(inside, full, 0.0).astype(BF16)

    @pl.loop(0, rows)
    def _(source):
        for t in range(3):
            for k in range(kernels):
                put(tb, (source + t) * 3 + t, k, near_block(fr[k, t, pl.ds(source, 1), 0:256]))

    forward.pass_on(2)
    for pole in (0, 1):

        @pl.when(north if pole == 0 else south)
        def _():
            for a in range(4):
                row = a if pole == 0 else rows - 1 - a
                for t in range(3):
                    for k in range(kernels):
                        put(te, a * 3 + t, k, far_block(ff, row, t, k))
                        put(tbe, a * 3 + t, k, far_block(fr, row, t, k))

    @pl.when(below)
    def _():
        filter_copy(-1).wait_recv()

    @pl.when(above)
    def _():
        filter_copy(1).wait_recv()

    for k in range(kernels):
        put(tb, 3 + 2, k, near_block(frecv[1, k : k + 1, 0:256]))
        put(tb, rows * 3, k, near_block(frecv[0, k : k + 1, 0:256]))

    for copy in locals_[2:]:
        copy.wait()

    def far_term(table, index, buf, row, both):
        if both:
            return jnp.dot(table[index], buf[row], preferred_element_type=F32)
        return jnp.dot(
            table[index, :, lon_dev : 3 * lon_dev],
            buf[row, lon_dev : 3 * lon_dev, :],
            preferred_element_type=F32,
        )

    def rows_in(span):
        return [first + n for first, count in span for n in range(count)]

    def scatter(ref, span, shift, at, value):
        done = 0
        for first, count in span:
            piece = value[done * lon_dev : (done + count) * lon_dev]
            ref[pl.ds(first + shift, count), at, :] = piece.reshape(count, lon_dev, channels)
            done += count

    def conv(table, offset, buf, shift, flipped, span):
        for n, i in enumerate(rows_in(span)):
            total = None
            for t in range(3):
                row = i + (2 - t if flipped else t)
                term = jnp.dot(
                    table[(i + offset) * 3 + t, :, 0:wide], buf[row], preferred_element_type=F32
                )
                total = term if total is None else total + term
            acc[n] = total

    def far_conv(table, buf, flipped, span):
        for pole in (0, 1):
            found = []
            for n, i in enumerate(rows_in(span)):
                for t in range(3):
                    source = i + (1 - t if flipped else t - 1)
                    away = source if pole == 0 else rows - 1 - source
                    a = i if pole == 0 else rows - 1 - i
                    filter_row = away if flipped else a
                    if 0 <= filter_row < 4 and away >= 0:
                        found.append((n, filter_row, t, source))
            if not found:
                continue

            @pl.when(north if pole == 0 else south)
            def _():
                for n, a, t, source in found:
                    acc[n] += far_term(table, a * 3 + t, buf, source + 1, a < 2)

    def gather(span):
        count = len(rows_in(span))
        for n in range(count):
            for k in range(kernels):
                cv[pl.ds(n * lon_dev, lon_dev), pl.ds(k * channels, channels)] = acc[
                    n, pl.ds(k * lon_dev, lon_dev), :
                ].astype(BF16)
        return pl.ds(0, count * lon_dev)

    root = 0.7978845608028654
    cubic = 0.044715

    def forward_rows(span):
        conv(tf, 0, xw, 0, False, span)
        far_conv(te, xe, False, span)
        at = gather(span)
        mixed = jnp.dot(cv[at, :], wbd[...], preferred_element_type=F32).astype(BF16)
        v = jnp.dot(mixed, wm[...], preferred_element_type=F32)
        square = v * v
        th = jnp.tanh(root * v * (1.0 + cubic * square))
        half = 0.5 * (1.0 + th)
        slope = half + 0.5 * v * (1.0 - th * th) * (root * (1.0 + 3.0 * cubic * square))
        pull = jnp.concatenate(
            [go[pl.ds(first, n)].reshape(n * lon_dev, channels) for first, n in span], axis=0
        )
        pulled = pull.astype(F32) * slope
        back = lax.dot_general(
            pulled.astype(BF16), wm[...], (((1,), (1,)), ((), ())), preferred_element_type=F32
        )
        scatter(gw, span, 1, own, back.astype(BF16))
        scatter(out_ref, span, 0, every, (v * half).astype(BF16))

    def backward_rows(span):
        conv(tb, 1, gw, 0, True, span)
        far_conv(tbe, ge, True, span)
        at = gather(span)
        total = None
        for k in range(kernels):
            lanes = pl.ds(k * channels, channels)
            term = lax.dot_general(
                cv[at, lanes], wbd[lanes, :], (((1,), (1,)), ((), ())), preferred_element_type=F32
            )
            total = term if total is None else total + term
        scatter(gin_ref, span, 0, every, total.astype(BF16))

    def finish(phase):
        for g in range(3):
            phase.sent(g)
        phase.lifts("wait_send")
        for up in (-1, 1):
            phase.spreads(up, "wait_send")
        for pole in (0, 1):
            for early in (True, False):
                phase.fars(pole, early, "wait_send")

    outer, middle = ((0, 2), (6, 2)), ((2, 4),)
    forward.arrive(0)
    forward.arrive(1)
    for up in (1, -1):
        forward.spreads(up, "wait_recv")
    for pole in (0, 1):
        forward.fars(pole, True, "wait_recv")
    forward_rows(outer)

    @pl.when(above)
    def _():
        run(backward.lift(-1), "start")

    @pl.when(below)
    def _():
        run(backward.lift(1), "start")

    run(backward.group(0), "start")
    run(backward.group(1), "start")
    forward.arrive(2)
    for pole in (0, 1):
        forward.fars(pole, False, "wait_recv")
    forward_rows(middle)
    for pole in (0, 1):
        backward.fars(pole, False, "start")
    run(backward.group(2), "start")
    backward.lifts("wait_recv")
    for up in (-1, 1):
        backward.spreads(up, "start")
    backward.pass_on(0)
    for pole in (0, 1):
        backward.fars(pole, True, "start")
    backward.pass_on(1)
    finish(forward)

    @pl.when(above)
    def _():
        filter_copy(-1).wait_send()

    @pl.when(below)
    def _():
        filter_copy(1).wait_send()

    backward.pass_on(2)
    for g in range(3):
        backward.arrive(g)
    for early in (True, False):
        for pole in (0, 1):
            backward.fars(pole, early, "wait_recv")
    backward_rows(middle)
    for up in (1, -1):
        backward.spreads(up, "wait_recv")
    backward_rows(outer)
    finish(backward)


def body(n_lon, n_lat, inputs, psi_raw, widths, w_group, w_mix, grad_out):
    rows, lon_dev, channels = inputs.shape
    kernels = psi_raw.shape[0]
    wide = 5 * lon_dev
    depth = kernels * lon_dev
    copies = 30
    psi_raw = jnp.transpose(psi_raw, (0, 2, 1, 3))
    anywhere = pl.BlockSpec(memory_space=pltpu.HBM)
    vmem = pl.BlockSpec(memory_space=pltpu.VMEM)
    shape = jax.ShapeDtypeStruct(inputs.shape, BF16)
    both = pl.pallas_call(
        functools.partial(kernel, n_lon, n_lat),
        name="disco",
        out_shape=pltpu.VMEM((2,) + inputs.shape, BF16),
        in_specs=[
            anywhere, anywhere, pl.BlockSpec(memory_space=pltpu.SMEM),
            anywhere, anywhere, anywhere,
        ],
        out_specs=vmem,
        scratch_shapes=[
            pltpu.VMEM(psi_raw.shape, F32),
            pltpu.VMEM(w_group.shape, BF16),
            pltpu.VMEM(w_mix.shape, BF16),
            pltpu.VMEM(grad_out.shape, BF16),
            pltpu.VMEM((rows + 2, wide, channels), BF16),
            pltpu.VMEM((rows + 2, wide, channels), BF16),
            pltpu.VMEM((rows + 2, 4 * lon_dev, channels), BF16),
            pltpu.VMEM((rows + 2, 4 * lon_dev, channels), BF16),
            pltpu.VMEM((kernels, 3, rows, LANES), F32),
            pltpu.VMEM((kernels, 3, rows, LANES), F32),
            pltpu.VMEM((2, 8, LANES), F32),
            pltpu.VMEM((2, 8, LANES), F32),
            pltpu.VMEM((rows * 3, depth, 256), BF16),
            pltpu.VMEM(((rows + 2) * 3, depth, 256), BF16),
            pltpu.VMEM((12, depth, 4 * lon_dev), BF16),
            pltpu.VMEM((12, depth, 4 * lon_dev), BF16),
            pltpu.VMEM((kernels * channels, channels), BF16),
            pltpu.VMEM((4 * lon_dev, kernels * channels), BF16),
            pltpu.VMEM((4, depth, channels), F32),
            pltpu.SemaphoreType.DMA((5,)),
            pltpu.SemaphoreType.DMA((2, copies)),
            pltpu.SemaphoreType.DMA((2, copies)),
        ],
        compiler_params=pltpu.CompilerParams(
            collective_id=0, has_side_effects=True
        ),
        cost_estimate=pl.CostEstimate(
            flops=4_000_000_000, bytes_accessed=2_000_000, transcendentals=65536
        ),
    )(inputs, psi_raw, widths, w_group, w_mix, grad_out)
    return both[0], both[1]


def solution(mesh):
    return jax.shard_map(
        functools.partial(body, mesh.shape["lon"], mesh.shape["lat"]),
        mesh=mesh,
        in_specs=(
            P("lat", "lon", None),
            P(None, "lat", None, None),
            P("lat"),
            P(),
            P(),
            P("lat", "lon", None),
        ),
        out_specs=(P("lat", "lon", None), P("lat", "lon", None)),
        check_vma=False,
    )
```

```python
import functools

import jax
import jax.numpy as jnp
from jax import lax
from jax.experimental import pallas as pl
from jax.experimental.pallas import tpu as pltpu
from jax.sharding import PartitionSpec as P

GROUP = 4
SMAX = 4
LANES = 384
NEAR = (-1, 1, -2, 2)
SLOT = {-2: 0, -1: 1, 0: 2, 1: 3, 2: 4}
FAR_SLOT = {-4: 0, -3: 1, 3: 2, 4: 3}
MESH = pl.DeviceIdType.MESH
F32 = jnp.float32
BF16 = jnp.bfloat16


def iota(shape, axis):
    return lax.broadcasted_iota(jnp.int32, shape, axis)


def kernel(
    n_lon, n_lat,
    x_hbm, psi_hbm, widths, wg_hbm, wm_hbm, go_hbm,
    both_ref,
    psi, wg, wm, go, xw, gw, xe, ge, ff, fr, fsend, frecv, tf, tb, te, tbe, wbd, cv, acc,
    local_sem, send_sem, recv_sem,
):
    out_ref, gin_ref = both_ref.at[0], both_ref.at[1]
    rows, lon_dev, channels = x_hbm.shape
    kernels, taps = psi_hbm.shape[0], psi_hbm.shape[3]
    centre = SMAX * lon_dev
    wide = lon_dev * 5
    lon, lat = lax.axis_index("lon"), lax.axis_index("lat")
    north, south = lat == 0, lat == n_lat - 1
    above, below = jnp.logical_not(north), jnp.logical_not(south)

    def at_lon(by):
        return lax.rem(lon + (by + n_lon), n_lon)

    barrier = pltpu.get_barrier_semaphore()

    def greet(by, up):
        pl.semaphore_signal(
            barrier, inc=1, device_id={"lon": at_lon(by), "lat": lat + up}, device_id_type=MESH
        )

    for by in NEAR:
        greet(by, 0)

    @pl.when(above)
    def _():
        greet(0, -1)

    @pl.when(below)
    def _():
        greet(0, 1)

    polar = jnp.logical_or(north, south)

    @pl.when(polar)
    def _():
        for by in (-3, 3):
            greet(by, 0)

    own = pl.ds(SLOT[0] * lon_dev, lon_dev)
    every = pl.ds(0, lon_dev)
    locals_ = [
        pltpu.make_async_copy(psi_hbm, psi, local_sem.at[0]),
        pltpu.make_async_copy(wg_hbm, wg, local_sem.at[1]),
        pltpu.make_async_copy(wm_hbm, wm, local_sem.at[2]),
        pltpu.make_async_copy(go_hbm, go, local_sem.at[3]),
        pltpu.make_async_copy(x_hbm, xw.at[pl.ds(1, rows), own, :], local_sem.at[4]),
    ]
    for copy in locals_:
        copy.start()

    side = 1 - 2 * lax.rem(lon, 2)

    def slot_at(by):
        return pl.ds(pl.multiple_of((by + 2) * lon_dev, lon_dev), lon_dev)

    def remote(phase, index, src, dst, by, up=0):
        return pltpu.make_async_remote_copy(
            src_ref=src,
            dst_ref=dst,
            send_sem=send_sem.at[phase, index],
            recv_sem=recv_sem.at[phase, index],
            device_id={"lon": at_lon(by), "lat": lat + up},
            device_id_type=MESH,
        )

    def slot(by):
        return pl.ds(SLOT[by] * lon_dev, lon_dev)

    def far_slot(by):
        return pl.ds(FAR_SLOT[by] * lon_dev, lon_dev)

    class Phase:
        def __init__(self, phase, source, first, at, buf, far_buf, groups, far_count, routes):
            self.phase, self.source, self.first, self.at = phase, source, first, at
            self.buf, self.far_buf, self.groups = buf, far_buf, groups
            self.far_count, self.routes = far_count, routes

        def first_of(self, g):
            row, count = self.groups[g]
            return jnp.where(south, rows - row - count, row)

        def rows_of(self, row, count):
            return self.source.at[pl.ds(self.first + row, count), self.at, :]

        def part(self, g, n, by, at):
            row, count = self.first_of(g), self.groups[g][1]
            return remote(
                self.phase, g * 4 + n, self.rows_of(row, count),
                self.buf.at[pl.ds(1 + row, count), at, :], by,
            )

        def group(self, g):
            found = [
                self.part(g, 0, side, slot_at(-side)),
                self.part(g, 2, -2 * side, slot_at(2 * side)),
                self.part(g, 3, 2 * side, slot_at(-2 * side)),
            ]
            if self.routes[g] is None:
                found.insert(0, self.part(g, 1, -side, slot_at(side)))
            return found

        def relay(self, g):
            rows_ = pl.ds(1 + self.first_of(g), self.groups[g][1])
            if self.routes[g] == "plane":
                source, target, by = side, -side, 2 * side
            else:
                source, target, by = 2 * side, side, side
            return [
                remote(
                    self.phase, g * 4 + 1, self.buf.at[rows_, slot_at(source), :],
                    self.buf.at[rows_, slot_at(target), :], by,
                )
            ]

        def landed(self, g, which):
            ats = {0: side, 1: -side, 2: 2 * side, 3: -2 * side}
            return [self.part(g, n, side, slot_at(ats[n])) for n in which]

        def pass_on(self, g):
            run(self.landed(g, (0, 2, 3)), "wait_recv")
            if self.routes[g]:
                run(self.relay(g), "start")

        def arrive(self, g):
            run(self.landed(g, (1,)), "wait_recv")

        def sent(self, g):
            run(self.group(g), "wait_send")
            if self.routes[g]:
                run(self.relay(g), "wait_send")

        def lift(self, up):
            row, target = (0, rows + 1) if up < 0 else (rows - 1, 0)
            return [
                remote(
                    self.phase, 12 + (0 if up < 0 else 1), self.rows_of(row, 1),
                    self.buf.at[pl.ds(target, 1), own, :], 0, up,
                )
            ]

        def spread(self, up):
            target = rows + 1 if up < 0 else 0
            return [
                remote(
                    self.phase, 14 + n + (0 if up < 0 else 4),
                    self.buf.at[pl.ds(target, 1), own, :],
                    self.buf.at[pl.ds(target, 1), slot(-by), :], by,
                )
                for n, by in enumerate(NEAR)
            ]

        def far(self, pole, early):
            count = self.far_count
            if early:
                rows_ = pl.ds(1 if pole == 0 else 1 + rows - count, count)
                return [
                    remote(
                        self.phase, 22 + 2 * (reach - 3) + (s + 1) // 2,
                        self.buf.at[rows_, slot(2 * s), :],
                        self.far_buf.at[rows_, far_slot(s * reach), :], -s * (reach - 2),
                    )
                    for reach in (3, 4)
                    for s in (-1, 1)
                ]
            row = count if pole == 0 else rows - count - 2
            return [
                remote(
                    self.phase, 28 + (s + 1) // 2, self.rows_of(row, 2),
                    self.far_buf.at[pl.ds(1 + row, 2), far_slot(-3 * s), :], 3 * s,
                )
                for s in (-1, 1)
            ]

        def lifts(self, what):
            for up in (-1, 1):
                ok = (above if up < 0 else below) if what != "wait_recv" else (
                    below if up < 0 else above
                )

                @pl.when(ok)
                def _():
                    run(self.lift(up), what)

        def spreads(self, up, what):
            @pl.when(below if up < 0 else above)
            def _():
                run(self.spread(up), what)

        def fars(self, pole, early, what):
            @pl.when(north if pole == 0 else south)
            def _():
                run(self.far(pole, early), what)

    def run(copies, what):
        for copy in copies:
            getattr(copy, what)()

    forward = Phase(0, x_hbm, 0, every, xw, xe, ((0, 3), (5, 3), (3, 2)), 3, ('pair', 'plane', 'pair'))
    backward = Phase(1, gw, 1, own, gw, ge, ((0, 2), (6, 2), (2, 4)), 2, ('plane', 'plane', None))

    pl.semaphore_wait(
        barrier,
        4 + above.astype(jnp.int32) + below.astype(jnp.int32) + 2 * polar.astype(jnp.int32),
    )
    forward.lifts("start")
    run(forward.group(0), "start")
    run(forward.group(1), "start")

    locals_[0].wait()
    line = iota((rows, LANES), 0)
    reach = jnp.zeros((rows, LANES), jnp.int32)
    for i in range(rows):
        reach = jnp.where(line == i, widths[i] * lon_dev, reach)
    keep = jnp.where(
        jnp.abs(iota((rows, LANES), 1) - centre) <= reach,
        lax.rsqrt(3.0 * (2.0 * reach.astype(F32) + 1.0)),
        0.0,
    )
    ff[:, :, :, 256:LANES] = jnp.zeros((kernels, 3, rows, LANES - 256), F32)
    for k in range(kernels):
        for t in range(3):
            ff[k, t, :, 0:taps] = psi[k, t] * keep[:, 0:taps]


    forward.lifts("wait_recv")
    for up in (-1, 1):
        forward.spreads(up, "start")
    run(forward.group(2), "start")
    for pole in (0, 1):
        forward.fars(pole, False, "start")

    flip = jnp.where(
        iota((LANES, LANES), 0) + iota((LANES, LANES), 1) == 2 * centre, 1.0, 0.0
    ).astype(BF16)
    flipped = jnp.dot(
        ff[...].reshape(3 * kernels * rows, LANES).astype(BF16), flip, preferred_element_type=F32
    )
    fr[...] = flipped.reshape(kernels, 3, rows, LANES)
    for k in range(kernels):
        fsend[0, k : k + 1, :] = fr[k, 0, 0:1, :]
        fsend[1, k : k + 1, :] = fr[k, 2, rows - 1 : rows, :]

    def filter_copy(up):
        n = 0 if up < 0 else 1
        return remote(0, 26 + n, fsend.at[n], frecv.at[n], 0, up)

    @pl.when(above)
    def _():
        filter_copy(-1).start()

    @pl.when(below)
    def _():
        filter_copy(1).start()

    blank = jnp.zeros((wide, channels), BF16)

    @pl.when(north)
    def _():
        xw[0] = blank
        gw[0] = blank
        frecv[1] = jnp.zeros(frecv.shape[1:], F32)

    @pl.when(south)
    def _():
        xw[rows + 1] = blank
        gw[rows + 1] = blank
        frecv[0] = jnp.zeros(frecv.shape[1:], F32)

    def near_block(base):
        base = jnp.broadcast_to(base, (lon_dev, 256))
        return pltpu.roll(base, 256 - 2 * lon_dev, 1, stride=1, stride_axis=0).astype(BF16)

    def far_block(filters, row, t, k):
        lane = iota((lon_dev, 128), 1)

        def part(first):
            return jnp.broadcast_to(
                filters[k, t, row : row + 1, first : first + 128], (lon_dev, 128)
            )

        low = jnp.where(lane < 2 * lon_dev, part(0), 0.0)
        high = jnp.where(lane > 2 * lon_dev, part(128), part(256))
        low = pltpu.roll(low, 0, 1, stride=1, stride_axis=0)
        high = pltpu.roll(high, 128 - lon_dev, 1, stride=1, stride_axis=0)
        return jnp.where(lane < 2 * lon_dev, low, high).astype(BF16)

    def put(dst, index, k, block):
        dst[index, pl.ds(k * lon_dev, lon_dev), :] = block

    @pl.loop(0, rows)
    def _(i):
        for t in range(3):
            for k in range(kernels):
                put(tf, i * 3 + t, k, near_block(ff[k, t, pl.ds(i, 1), 0:256]))

    forward.pass_on(0)
    for pole in (0, 1):
        forward.fars(pole, True, "start")
    forward.pass_on(1)

    locals_[1].wait()
    inside = (iota((channels, channels), 0) // GROUP) == (iota((channels, channels), 1) // GROUP)
    for k in range(kernels):
        four = wg[k].astype(F32)
        eight = jnp.concatenate([four, four], axis=0)
        full = jnp.broadcast_to(eight[None], (channels // 8, 8, channels))
        full = full.reshape(channels, channels)
        wbd[pl.ds(k * channels, channels), :] = jnp.where(inside, full, 0.0).astype(BF16)

    @pl.loop(0, rows)
    def _(source):
        for t in range(3):
            for k in range(kernels):
                put(tb, (source + t) * 3 + t, k, near_block(fr[k, t, pl.ds(source, 1), 0:256]))

    forward.pass_on(2)
    for pole in (0, 1):

        @pl.when(north if pole == 0 else south)
        def _():
            for a in range(4):
                row = a if pole == 0 else rows - 1 - a
                for t in range(3):
                    for k in range(kernels):
                        put(te, a * 3 + t, k, far_block(ff, row, t, k))
                        put(tbe, a * 3 + t, k, far_block(fr, row, t, k))

    @pl.when(below)
    def _():
        filter_copy(-1).wait_recv()

    @pl.when(above)
    def _():
        filter_copy(1).wait_recv()

    for k in range(kernels):
        put(tb, 3 + 2, k, near_block(frecv[1, k : k + 1, 0:256]))
        put(tb, rows * 3, k, near_block(frecv[0, k : k + 1, 0:256]))

    for copy in locals_[2:]:
        copy.wait()

    def far_term(table, index, buf, row, both):
        if both:
            return jnp.dot(table[index], buf[row], preferred_element_type=F32)
        return jnp.dot(
            table[index, :, lon_dev : 3 * lon_dev],
            buf[row, lon_dev : 3 * lon_dev, :],
            preferred_element_type=F32,
        )

    def rows_in(span):
        return [first + n for first, count in span for n in range(count)]

    def scatter(ref, span, shift, at, value):
        done = 0
        for first, count in span:
            piece = value[done * lon_dev : (done + count) * lon_dev]
            ref[pl.ds(first + shift, count), at, :] = piece.reshape(count, lon_dev, channels)
            done += count

    def conv(table, offset, buf, shift, flipped, span):
        for n, i in enumerate(rows_in(span)):
            total = None
            for t in range(3):
                row = i + (2 - t if flipped else t)
                term = jnp.dot(
                    table[(i + offset) * 3 + t, :, 0:wide], buf[row], preferred_element_type=F32
                )
                total = term if total is None else total + term
            acc[n] = total

    def far_conv(table, buf, flipped, span):
        for pole in (0, 1):
            found = []
            for n, i in enumerate(rows_in(span)):
                for t in range(3):
                    source = i + (1 - t if flipped else t - 1)
                    away = source if pole == 0 else rows - 1 - source
                    a = i if pole == 0 else rows - 1 - i
                    filter_row = away if flipped else a
                    if 0 <= filter_row < 4 and away >= 0:
                        found.append((n, filter_row, t, source))
            if not found:
                continue

            @pl.when(north if pole == 0 else south)
            def _():
                for n, a, t, source in found:
                    acc[n] += far_term(table, a * 3 + t, buf, source + 1, a < 2)

    def gather(span):
        count = len(rows_in(span))
        for n in range(count):
            for k in range(kernels):
                cv[pl.ds(n * lon_dev, lon_dev), pl.ds(k * channels, channels)] = acc[
                    n, pl.ds(k * lon_dev, lon_dev), :
                ].astype(BF16)
        return pl.ds(0, count * lon_dev)

    root = 0.7978845608028654
    cubic = 0.044715

    def forward_rows(span):
        conv(tf, 0, xw, 0, False, span)
        far_conv(te, xe, False, span)
        at = gather(span)
        mixed = jnp.dot(cv[at, :], wbd[...], preferred_element_type=F32).astype(BF16)
        v = jnp.dot(mixed, wm[...], preferred_element_type=F32)
        square = v * v
        th = jnp.tanh(root * v * (1.0 + cubic * square))
        half = 0.5 * (1.0 + th)
        slope = half + 0.5 * v * (1.0 - th * th) * (root * (1.0 + 3.0 * cubic * square))
        pull = jnp.concatenate(
            [go[pl.ds(first, n)].reshape(n * lon_dev, channels) for first, n in span], axis=0
        )
        pulled = pull.astype(F32) * slope
        back = lax.dot_general(
            pulled.astype(BF16), wm[...], (((1,), (1,)), ((), ())), preferred_element_type=F32
        )
        scatter(gw, span, 1, own, back.astype(BF16))
        scatter(out_ref, span, 0, every, (v * half).astype(BF16))

    def backward_rows(span):
        conv(tb, 1, gw, 0, True, span)
        far_conv(tbe, ge, True, span)
        at = gather(span)
        total = None
        for k in range(kernels):
            lanes = pl.ds(k * channels, channels)
            term = lax.dot_general(
                cv[at, lanes], wbd[lanes, :], (((1,), (1,)), ((), ())), preferred_element_type=F32
            )
            total = term if total is None else total + term
        scatter(gin_ref, span, 0, every, total.astype(BF16))

    def finish(phase):
        for g in range(3):
            phase.sent(g)
        phase.lifts("wait_send")
        for up in (-1, 1):
            phase.spreads(up, "wait_send")
        for pole in (0, 1):
            for early in (True, False):
                phase.fars(pole, early, "wait_send")

    outer, middle = ((0, 2), (6, 2)), ((2, 4),)
    forward.arrive(0)
    forward.arrive(1)
    for up in (1, -1):
        forward.spreads(up, "wait_recv")
    for pole in (0, 1):
        forward.fars(pole, True, "wait_recv")
    forward_rows(outer)

    @pl.when(above)
    def _():
        run(backward.lift(-1), "start")

    @pl.when(below)
    def _():
        run(backward.lift(1), "start")

    run(backward.group(0), "start")
    run(backward.group(1), "start")
    forward.arrive(2)
    for pole in (0, 1):
        forward.fars(pole, False, "wait_recv")
    forward_rows(middle)
    for pole in (0, 1):
        backward.fars(pole, False, "start")
    run(backward.group(2), "start")
    backward.lifts("wait_recv")
    for up in (-1, 1):
        backward.spreads(up, "start")
    backward.pass_on(0)
    for pole in (0, 1):
        backward.fars(pole, True, "start")
    backward.pass_on(1)
    finish(forward)

    @pl.when(above)
    def _():
        filter_copy(-1).wait_send()

    @pl.when(below)
    def _():
        filter_copy(1).wait_send()

    backward.pass_on(2)
    for g in range(3):
        backward.arrive(g)
    for early in (True, False):
        for pole in (0, 1):
            backward.fars(pole, early, "wait_recv")
    backward_rows(middle)
    for up in (1, -1):
        backward.spreads(up, "wait_recv")
    backward_rows(outer)
    finish(backward)


def body(n_lon, n_lat, inputs, psi_raw, widths, w_group, w_mix, grad_out):
    rows, lon_dev, channels = inputs.shape
    kernels = psi_raw.shape[0]
    wide = 5 * lon_dev
    depth = kernels * lon_dev
    copies = 30
    psi_raw = jnp.transpose(psi_raw, (0, 2, 1, 3))
    anywhere = pl.BlockSpec(memory_space=pltpu.HBM)
    vmem = pl.BlockSpec(memory_space=pltpu.VMEM)
    shape = jax.ShapeDtypeStruct(inputs.shape, BF16)
    both = pl.pallas_call(
        functools.partial(kernel, n_lon, n_lat),
        name="disco",
        out_shape=pltpu.VMEM((2,) + inputs.shape, BF16),
        in_specs=[
            anywhere, anywhere, pl.BlockSpec(memory_space=pltpu.SMEM),
            anywhere, anywhere, anywhere,
        ],
        out_specs=vmem,
        scratch_shapes=[
            pltpu.VMEM(psi_raw.shape, F32),
            pltpu.VMEM(w_group.shape, BF16),
            pltpu.VMEM(w_mix.shape, BF16),
            pltpu.VMEM(grad_out.shape, BF16),
            pltpu.VMEM((rows + 2, wide, channels), BF16),
            pltpu.VMEM((rows + 2, wide, channels), BF16),
            pltpu.VMEM((rows + 2, 4 * lon_dev, channels), BF16),
            pltpu.VMEM((rows + 2, 4 * lon_dev, channels), BF16),
            pltpu.VMEM((kernels, 3, rows, LANES), F32),
            pltpu.VMEM((kernels, 3, rows, LANES), F32),
            pltpu.VMEM((2, 8, LANES), F32),
            pltpu.VMEM((2, 8, LANES), F32),
            pltpu.VMEM((rows * 3, depth, 256), BF16),
            pltpu.VMEM(((rows + 2) * 3, depth, 256), BF16),
            pltpu.VMEM((12, depth, 4 * lon_dev), BF16),
            pltpu.VMEM((12, depth, 4 * lon_dev), BF16),
            pltpu.VMEM((kernels * channels, channels), BF16),
            pltpu.VMEM((4 * lon_dev, kernels * channels), BF16),
            pltpu.VMEM((4, depth, channels), F32),
            pltpu.SemaphoreType.DMA((5,)),
            pltpu.SemaphoreType.DMA((2, copies)),
            pltpu.SemaphoreType.DMA((2, copies)),
        ],
        compiler_params=pltpu.CompilerParams(
            collective_id=0, has_side_effects=True
        ),
        cost_estimate=pl.CostEstimate(
            flops=4_000_000_000, bytes_accessed=2_000_000, transcendentals=65536
        ),
    )(inputs, psi_raw, widths, w_group, w_mix, grad_out)
    return both[0], both[1]


def solution(mesh):
    return jax.shard_map(
        functools.partial(body, mesh.shape["lon"], mesh.shape["lat"]),
        mesh=mesh,
        in_specs=(
            P("lat", "lon", None),
            P(None, "lat", None, None),
            P("lat"),
            P(),
            P(),
            P("lat", "lon", None),
        ),
        out_specs=(P("lat", "lon", None), P("lat", "lon", None)),
        check_vma=False,
    )
```
